128 devices in a mesh: alpha: 16 (over x_lo, z, core), beta: 8 (over x_hi, y).
Axes of the slice: x: 4 (x_hi: 2, x_lo: 2; x = x_hi * 2 + x_lo), y: 4, z: 4, core: 2. Of those that a mesh axis runs over, the one named last changes fastest.
Arguments:
- coefficients: bfloat16 [8192, 8192], P('alpha', 'beta'), may hold values from -6 to 6
- diagonal: float32 [8192, 8192], P('alpha', 'beta'), may hold values from 0.5 to 2
- alpha_blocks: bfloat16 [64, 14, 128, 128], P('alpha'), may hold values from -0.125 to 0.125
- alpha_lists: int32 [64, 14], replicated, may hold values from 0 to 63, as said below
- beta_blocks: bfloat16 [64, 14, 128, 128], P('beta'), may hold values from -0.125 to 0.125
- beta_lists: int32 [64, 14], replicated, may hold values from 0 to 63, as said below
Outputs:
- sigma_out: bfloat16 [8192, 8192], P('alpha', 'beta')
The draws below stay inside these ranges and needn't reach their ends.
Inputs may be any that keep to these rules, and one draw needn't show every extreme that they name: `alpha_lists`: each row names 14 different blocks. For every alpha device, the rows of its 4 block rows name at most 2 different blocks owned by any one alpha device (blocks j * 4 to (j + 1) * 4 - 1 belong to device j), and exactly 2 from some owner. `beta_lists`: each row names 14 different blocks. For every beta device, the rows of its 8 block rows name at most 4 different blocks owned by any one beta device (blocks j * 8 to (j + 1) * 8 - 1 belong to device j), and exactly 4 from some owner.
All inputs are finite; a program needn't handle non-finite values.
Results may differ from the reference program's by a relative error of at most 0.001.
Values may be sent and summed in bfloat16 or wider, within the bound.
A program may use at most 128 MiB of HBM per device.

```python
import jax
import jax.numpy as jnp
from jax import lax

BLK = 128
SLOTS = 14
RA = 4
RB = 8
CAP_A = 2
CAP_B = 4
NBR_A = 64
NBR_B = 64
NA = 8192
NB = 8192


def draw_lists(key, owners, per_owner, limit):
    key_pick, key_rows, key_force = jax.random.split(key, 3)
    order_scores = jax.random.randint(key_pick, (owners, owners, per_owner), 0, 2 ** 20) * per_owner + jnp.arange(per_owner, dtype=jnp.int32)
    order = jnp.argsort(order_scores, axis=-1)[..., :limit].astype(jnp.int32)
    candidates = (jnp.arange(owners, dtype=jnp.int32)[None, :, None] * per_owner + order).reshape(owners, owners * limit)
    total = owners * limit
    forced = jax.random.randint(key_force, (owners,), 0, owners)
    position = jnp.arange(total, dtype=jnp.int32)
    row_scores = jax.random.randint(key_rows, (owners, per_owner, total), 0, 2 ** 20) * total + position
    force_mask = (jnp.arange(per_owner)[None, :, None] == 0) & ((position // limit)[None, None, :] == forced[:, None, None])
    row_scores = jnp.where(force_mask, position - total, row_scores)
    picks = jnp.argsort(row_scores, axis=-1)[..., :SLOTS]
    spread = jnp.broadcast_to(candidates[:, None, :], (owners, per_owner, total))
    chosen = jnp.take_along_axis(spread, picks, axis=-1)
    return chosen.reshape(owners * per_owner, SLOTS).astype(jnp.int32)


def draw_alpha_lists(key, part):
    return draw_lists(jax.random.fold_in(key, 11), NBR_A // RA, RA, CAP_A)


def draw_beta_lists(key, part):
    return draw_lists(jax.random.fold_in(key, 23), NBR_B // RB, RB, CAP_B)


def block_scale(key, dims, pieces, smallest, largest):
    factor_of = 1.0
    for dim, blocks in pieces:
        draws = jax.random.uniform(jax.random.fold_in(jax.random.fold_in(key, 6), dim), (blocks,), jnp.float32, smallest / len(pieces), largest / len(pieces))
        factor_of = factor_of * jnp.repeat(jnp.exp(draws), dims[dim] // blocks).reshape((-1,) + (1,) * (len(dims) - 1 - dim))
    return factor_of


def scatter_about(own_key, extent, width, most, cuts=(), held_as=jnp.bfloat16):
    gain = block_scale(own_key, extent, cuts, -0.22, 0.18) if cuts else 1.0
    array = jax.random.normal(own_key, extent, jnp.float32) * width * gain
    return jnp.minimum(jnp.maximum(array, -most), most).astype(held_as)


def setup_inputs(seed: int = 0) -> dict:
    keys = jax.random.split(jax.random.key(seed), 7)
    coefficients = scatter_about(keys[0], (NA, NB), 1.0, 6.0, ((0, 16), (1, 8)))
    diagonal = jnp.clip(0.5 + 1.5 * jax.random.uniform(keys[1], (NA, NB), jnp.float32) ** block_scale(keys[1], (NA, NB), ((0, 16), (1, 8)), -0.2, 0.2), 0.5, 2.0)
    alpha_blocks = scatter_about(keys[2], (NBR_A, SLOTS, BLK, BLK), (SLOTS * BLK) ** -0.5, 0.125, ((0, 16),))
    alpha_lists = draw_alpha_lists(jax.random.fold_in(keys[6], 71), 0)
    beta_blocks = scatter_about(keys[4], (NBR_B, SLOTS, BLK, BLK), (SLOTS * BLK) ** -0.5, 0.125, ((0, 8),))
    beta_lists = draw_beta_lists(jax.random.fold_in(keys[6], 71), 0)
    return dict(coefficients=coefficients, diagonal=diagonal, alpha_blocks=alpha_blocks, alpha_lists=alpha_lists, beta_blocks=beta_blocks, beta_lists=beta_lists)


def alpha_part(coefficients, alpha_blocks, alpha_lists):
    stacked = coefficients.astype(jnp.float32).reshape(NBR_A, BLK, NB)

    def one_row(row_args):
        blocks_here, list_ids = row_args
        fetched = jnp.take(stacked, list_ids, axis=0)
        return jnp.einsum("kab,kbn->an", blocks_here.astype(jnp.float32), fetched)

    rows_out = lax.map(one_row, (alpha_blocks, alpha_lists))
    return rows_out.reshape(NA, NB)


def beta_part(coefficients, beta_blocks, beta_lists):
    stacked = coefficients.astype(jnp.float32).reshape(NA, NBR_B, BLK)

    def one_col(col_args):
        blocks_here, list_ids = col_args
        fetched = jnp.take(stacked, list_ids, axis=1)
        return jnp.einsum("mkb,kab->ma", fetched, blocks_here.astype(jnp.float32))

    cols_out = lax.map(one_col, (beta_blocks, beta_lists))
    return jnp.transpose(cols_out, (1, 0, 2)).reshape(NA, NB)


def reference(coefficients, diagonal, alpha_blocks, alpha_lists, beta_blocks, beta_lists):
    alpha_term = alpha_part(coefficients, alpha_blocks, alpha_lists)
    beta_term = beta_part(coefficients, beta_blocks, beta_lists)
    total = alpha_term + beta_term + diagonal * coefficients.astype(jnp.float32)
    return total.astype(jnp.bfloat16)
```

```python
import functools

import jax
import jax.numpy as jnp
from jax import lax
from jax.experimental import pallas as pl
from jax.experimental.pallas import tpu as pltpu
from jax.sharding import PartitionSpec as P

MESH = pl.DeviceIdType.MESH
BLK = 128
SLOTS = 14
RA = 4
RB = 8
CAP_A = 2
CAP_B = 4
ROWS = RA * BLK
COLS = RB * BLK

PIECES = {"n0": (0, 9), "n1": (9, 9), "f0": (18, 7), "f1": (25, 7)}
GROUPS = ROWS // 16
PER = BLK // 16
COMPUTE = True


def body(sel_a, inv_a, sel_b, inv_b, c_hbm, diag_hbm, ab_hbm, bb_hbm, out_ref, *scratch):
    it = iter(scratch)
    own, own_cb, peer_cb = next(it), next(it), next(it)
    gathered = {}
    for dx in range(2):
        for dz in range(4):
            for dc in range(2):
                if (dx, dz, dc) != (0, 0, 0):
                    gathered[dx, dz, dc] = next(it)
    peer = next(it)
    message = {(q, dy): next(it) for q in range(2) for dy in (1, 2, 3)}
    relay = {(q, up): next(it) for q in range(2) for up in range(2)}
    staged = {(q, dy): next(it) for q in range(2) for dy in (1, 2, 3)}
    ablk, bblk, diag, acc, wa, wb, xa, xb, send_sems, recv_sems, local_sems = it

    ia, ib = lax.axis_index("alpha"), lax.axis_index("beta")
    x_lo, z, core = ia // 8, (ia // 2) % 4, ia % 2
    x_hi, y = ib // 4, ib % 4

    def alpha_at(dx, dz, dc):
        return ((x_lo + dx) % 2) * 8 + ((z + dz) % 4) * 2 + (core + dc) % 2

    def beta_at(dxh, dy):
        return ((x_hi + dxh) % 2) * 4 + (y + dy) % 4

    target = {
        "s": (alpha_at(0, 0, 1), ib),
        "xi": (alpha_at(1, 0, 0), ib),
        "xo": (alpha_at(1, 0, 0), beta_at(1, 0)),
        "z+": (alpha_at(0, 1, 0), ib),
        "z-": (alpha_at(0, 3, 0), ib),
        "y+": (ia, beta_at(0, 1)),
        "y-": (ia, beta_at(0, 3)),
    }
    count = [0]
    started = []

    def send(link, src, dst):
        n = count[0]
        count[0] += 1
        copy = pltpu.make_async_remote_copy(
            src_ref=src,
            dst_ref=dst,
            send_sem=send_sems.at[n],
            recv_sem=recv_sems.at[n],
            device_id=target[link],
            device_id_type=MESH,
        )
        copy.start()
        started.append(copy)
        return copy

    def rows(ref, piece):
        first, size = PIECES[piece]
        return ref.at[pl.ds(first, size)]

    load_own = pltpu.make_async_copy(c_hbm, own, local_sems.at[0])
    load_own.start()
    load_a = pltpu.make_async_copy(ab_hbm, ablk.at[:, pl.ds(0, SLOTS)], local_sems.at[1])
    load_b = pltpu.make_async_copy(bb_hbm, bblk.at[:, pl.ds(0, SLOTS)], local_sems.at[2])
    load_d = pltpu.make_async_copy(diag_hbm, diag, local_sems.at[3])

    barrier = pltpu.get_barrier_semaphore()
    for link in target:
        pl.semaphore_signal(barrier, inc=1, device_id=target[link], device_id_type=MESH)
    load_b.start()
    load_a.start()
    load_d.start()
    pl.semaphore_wait(barrier, len(target))

    xi = {}
    zp = {}
    zm = {}
    sib = {}
    load_own.wait()
    for p in ("n0", "n1", "f0", "f1"):
        q = {"n0": "f0", "n1": "f1", "f0": "n0", "f1": "n1"}[p]
        xi[p] = send("xi", rows(own, p), rows(gathered[1, 0, 0], p))
        zp[q] = send("z+", rows(own, q), rows(gathered[0, 1, 0], q))
        zm[q] = send("z-", rows(own, q), rows(gathered[0, 3, 0], q))
    sib[0, 0] = [send("s", own, gathered[0, 0, 1])]

    def to_sibling(dx, dz, p):
        sib.setdefault((dx, dz), []).append(
            send("s", rows(gathered[dx, dz, 0], p), rows(gathered[dx, dz, 1], p))
        )

    def by_column(src, dst):
        def group(t, carry):
            for j in range(RB):
                dst[j, pl.ds(pl.multiple_of(t * 16, 16), 16), :] = src[t, :, j * BLK : (j + 1) * BLK]
            return carry

        lax.fori_loop(0, GROUPS, group, 0)

    def stage(q, src):
        for dy in (2, 1, 3):
            for s in range(CAP_B):
                at = sel_b[(beta_at(0, dy) % 4) * 8 + q * 4 + s]
                staged[q, dy][s] = src[at]

    sent_b = {}

    def send_staged(q):
        for up, link in enumerate(("y-", "y+")):
            half = staged[q, 2].at[pl.ds(up * 2, 2)]
            sent_b[q, "far", up] = send(link, half, relay[q, up])
        sent_b[q, 1] = send("y+", staged[q, 1], message[q, 1])
        sent_b[q, 3] = send("y-", staged[q, 3], message[q, 3])

    def pass_on(q):
        for up, link in enumerate(("y-", "y+")):
            sent_b[q, "far", up].wait_recv()
            sent_b[q, 2, up] = send(link, relay[q, up], message[q, 2].at[pl.ds(up * 2, 2)])

    def arrived_b(q, dy):
        if dy == 2:
            sent_b[q, 2, 0].wait_recv()
            sent_b[q, 2, 1].wait_recv()
        else:
            sent_b[q, dy].wait_recv()

    def alpha_chip(dx, dz):
        if not COMPUTE:
            return
        sources = [own if (dx, dz) == (0, 0) else gathered[dx, dz, 0], gathered[dx, dz, 1]]
        for dc in range(2):
            owner = alpha_at(dx, 4 - dz, dc)
            for s in range(CAP_A):
                for r in range(RA):
                    k = inv_a[r * 32 + owner * 2 + s]
                    wa[r * BLK : (r + 1) * BLK, (dc * 2 + s) * BLK : (dc * 2 + s + 1) * BLK] = ablk[r, k]
                pick = sel_a[owner * 2 + s] * PER
                for t in range(PER):
                    at = (dc * 2 + s) * BLK + t * 16
                    xa[at : at + 16, :] = sources[dc][pick + t]

        def tile(n, carry):
            cols = pl.ds(pl.multiple_of(n * 256, 256), 256)
            acc[:, cols] += jnp.dot(wa[...], xa[:, cols], preferred_element_type=jnp.float32)
            return carry

        lax.fori_loop(0, COLS // 256, tile, 0)

    def beta_owner(dxh, dy, load):
        if not COMPUTE:
            return
        owner = beta_at(dxh, 4 - dy)
        for s in range(CAP_B):
            for r in range(RB):
                k = inv_b[r * 32 + owner * 4 + s]
                wb[r * BLK : (r + 1) * BLK, s * BLK : (s + 1) * BLK] = bblk[r, k]
            load(s)

        def tile(n, carry):
            cols = pl.ds(pl.multiple_of(n * 256, 256), 256)
            acc[:, cols] += lax.dot_general(
                xb[...], wb[cols, :], (((1,), (1,)), ((), ())), preferred_element_type=jnp.float32
            )
            return carry

        lax.fori_loop(0, COLS // 256, tile, 0)

    def beta_local(q, src):
        def load(s):
            at = sel_b[y * 8 + q * 4 + s]
            xb[:, s * BLK : (s + 1) * BLK] = src[at]

        beta_owner(q, 0, load)

    def beta_message(q, dy):
        arrived_b(q, dy)

        def load(s):
            xb[:, s * BLK : (s + 1) * BLK] = message[q, dy][s]

        beta_owner(q, dy, load)

    by_column(own, own_cb)
    stage(0, own_cb)
    load_d.wait()

    def init(n, carry):
        at = pl.ds(pl.multiple_of(n * 64, 64), 64)
        acc[at, :] = diag[at, :] * own[pl.ds(n * 4, 4)].astype(jnp.float32).reshape(64, COLS)
        return carry

    lax.fori_loop(0, ROWS // 64, init, 0)
    for r in range(RA):
        ablk[r, SLOTS] = jnp.zeros((BLK, BLK), jnp.bfloat16)
    for r in range(RB):
        bblk[r, SLOTS] = jnp.zeros((BLK, BLK), jnp.bfloat16)
    send_staged(0)
    load_a.wait()
    load_b.wait()
    xf = {}
    xo = {}

    def z_first(p):
        zp[p].wait_recv()
        zm[p].wait_recv()
        for dz in (1, 3):
            xf[dz, p] = send("xi", rows(gathered[0, dz, 0], p), rows(gathered[1, dz, 0], p))
            to_sibling(0, dz, p)

    far = {}

    def forward(dx, p):
        if p in ("f0", "n0"):
            far[dx, p] = send("z+", rows(gathered[dx, 1, 0], p), rows(gathered[dx, 2, 0], p))
        else:
            far[dx, p] = send("z-", rows(gathered[dx, 3, 0], p), rows(gathered[dx, 2, 0], p))

    znp, znm = {}, {}

    def x_first(p, along_z):
        xi[p].wait_recv()
        xo[p] = send("xo", rows(gathered[1, 0, 0], p), rows(peer, p))
        if along_z:
            znp[p] = send("z+", rows(gathered[1, 0, 0], p), rows(gathered[1, 1, 0], p))
            znm[p] = send("z-", rows(gathered[1, 0, 0], p), rows(gathered[1, 3, 0], p))
        to_sibling(1, 0, p)

    z_first("f0")
    forward(0, "f0")
    x_first("n0", True)
    beta_local(0, own_cb)
    z_first("f1")
    forward(0, "f1")
    pass_on(0)
    x_first("n1", True)
    sib[0, 0][0].wait_recv()
    alpha_chip(0, 0)
    zp["n0"].wait_recv()
    zm["n0"].wait_recv()
    forward(0, "n0")
    to_sibling(0, 1, "n0")
    to_sibling(0, 3, "n0")
    x_first("f0", False)
    beta_message(0, 1)
    zp["n1"].wait_recv()
    zm["n1"].wait_recv()
    forward(0, "n1")
    to_sibling(0, 1, "n1")
    to_sibling(0, 3, "n1")
    x_first("f1", False)
    beta_message(0, 3)
    for p in ("f0", "f1"):
        far[0, p].wait_recv()
        xf[2, p] = send("xi", rows(gathered[0, 2, 0], p), rows(gathered[1, 2, 0], p))
        to_sibling(0, 2, p)
    for p in PIECES:
        xo[p].wait_recv()
    by_column(peer, peer_cb)
    stage(1, peer_cb)
    for s in sib[0, 1]:
        s.wait_recv()
    alpha_chip(0, 1)
    send_staged(1)
    for p in ("n0", "n1"):
        znp[p].wait_recv()
        znm[p].wait_recv()
        forward(1, p)
        to_sibling(1, 1, p)
        to_sibling(1, 3, p)
    for s in sib[0, 3]:
        s.wait_recv()
    alpha_chip(0, 3)
    beta_local(1, peer_cb)
    pass_on(1)
    beta_message(0, 2)
    for s in sib[1, 0]:
        s.wait_recv()
    alpha_chip(1, 0)
    for dz in (1, 3):
        for p in ("f0", "f1"):
            xf[dz, p].wait_recv()
            to_sibling(1, dz, p)
    beta_message(1, 1)
    beta_message(1, 3)
    for s in sib[1, 1]:
        s.wait_recv()
    alpha_chip(1, 1)
    for p in ("n0", "n1"):
        far[0, p].wait_recv()
        to_sibling(0, 2, p)
    for s in sib[1, 3]:
        s.wait_recv()
    alpha_chip(1, 3)
    for s in sib[0, 2]:
        s.wait_recv()
    alpha_chip(0, 2)
    beta_message(1, 2)
    for p in ("f0", "f1"):
        xf[2, p].wait_recv()
        to_sibling(1, 2, p)
    for p in ("n0", "n1"):
        far[1, p].wait_recv()
        to_sibling(1, 2, p)
    for s in sib[1, 2]:
        s.wait_recv()
    alpha_chip(1, 2)

    def finish(n, carry):
        at = pl.ds(pl.multiple_of(n * 64, 64), 64)
        out_ref[at, :] = acc[at, :].astype(jnp.bfloat16)
        return carry

    lax.fori_loop(0, ROWS // 64, finish, 0)
    for copy in started:
        copy.wait_send()
    assert count[0] <= NSEM


NSEM = 128


def picks_of(lists, owners, per_owner, cap):
    ids = owners[..., None] * per_owner + jnp.arange(per_owner, dtype=jnp.int32)
    flat = lists.reshape(lists.shape[:-2] + (-1,))
    needed = jnp.any(flat[..., None, None, :] == ids[..., None], axis=-1)
    before = jnp.arange(per_owner)[:, None] > jnp.arange(per_owner)[None, :]
    rank = jnp.sum(needed[..., None, :] & before, axis=-1)
    hit = needed[..., None, :] & (rank[..., None, :] == jnp.arange(cap)[:, None])
    position = jnp.arange(per_owner, dtype=jnp.int32)
    pick = jnp.max(jnp.where(hit, position, -1), axis=-1)
    return pick


def slots_of(lists, owners, picks, per_owner):
    wanted = jnp.where(picks >= 0, owners[:, None] * per_owner + picks, -1)
    same = lists[:, None, None, :] == wanted[None, :, :, None]
    return jnp.min(jnp.where(same, jnp.arange(SLOTS, dtype=jnp.int32), SLOTS), axis=-1)


def per_device(coefficients, diagonal, alpha_blocks, alpha_lists, beta_blocks, beta_lists):
    ia, ib = lax.axis_index("alpha"), lax.axis_index("beta")
    mine_a = lax.dynamic_slice_in_dim(alpha_lists, ia * RA, RA, 0)
    mine_b = lax.dynamic_slice_in_dim(beta_lists, ib * RB, RB, 0)
    owners_a = jnp.arange(16, dtype=jnp.int32)
    owners_b = jnp.arange(8, dtype=jnp.int32)
    pick_a = picks_of(mine_a, owners_a, RA, CAP_A)
    inv_a = slots_of(mine_a, owners_a, pick_a, RA)
    pick_b = picks_of(mine_b, owners_b, RB, CAP_B)
    inv_b = slots_of(mine_b, owners_b, pick_b, RB)
    column = lax.dynamic_slice_in_dim(beta_lists, (ib // 4) * 4 * RB, 4 * RB, 0).reshape(4, 1, RB, SLOTS)
    two = jnp.stack([ib, (ib + 4) % 8]).astype(jnp.int32)[None, :, None]
    send_b = picks_of(column, two, RB, CAP_B)
    sel_a = jnp.maximum(pick_a, 0).reshape(-1)
    sel_b = jnp.maximum(send_b, 0).reshape(-1)
    scratch = [pltpu.VMEM((GROUPS, 16, COLS), jnp.bfloat16)]
    scratch += [pltpu.VMEM((RB, ROWS, BLK), jnp.bfloat16) for _ in range(2)]
    scratch += [pltpu.VMEM((GROUPS, 16, COLS), jnp.bfloat16) for _ in range(16)]
    scratch += [pltpu.VMEM((CAP_B, ROWS, BLK), jnp.bfloat16) for _ in range(6)]
    scratch += [pltpu.VMEM((2, ROWS, BLK), jnp.bfloat16) for _ in range(4)]
    scratch += [pltpu.VMEM((CAP_B, ROWS, BLK), jnp.bfloat16) for _ in range(6)]
    scratch += [
        pltpu.VMEM((RA, SLOTS + 1, BLK, BLK), jnp.bfloat16),
        pltpu.VMEM((RB, SLOTS + 1, BLK, BLK), jnp.bfloat16),
        pltpu.VMEM((ROWS, COLS), jnp.float32),
        pltpu.VMEM((ROWS, COLS), jnp.float32),
        pltpu.VMEM((ROWS, 4 * BLK), jnp.bfloat16),
        pltpu.VMEM((COLS, 4 * BLK), jnp.bfloat16),
        pltpu.VMEM((4 * BLK, COLS), jnp.bfloat16),
        pltpu.VMEM((ROWS, 4 * BLK), jnp.bfloat16),
        pltpu.SemaphoreType.DMA((NSEM,)),
        pltpu.SemaphoreType.DMA((NSEM,)),
        pltpu.SemaphoreType.DMA((4,)),
    ]
    return pl.pallas_call(
        body,
        out_shape=jax.ShapeDtypeStruct((ROWS, COLS), jnp.bfloat16),
        in_specs=[pl.BlockSpec(memory_space=pltpu.SMEM)] * 4 + [pl.BlockSpec(memory_space=pl.ANY)] * 4,
        out_specs=pl.BlockSpec(memory_space=pltpu.VMEM),
        scratch_shapes=scratch,
        compiler_params=pltpu.CompilerParams(
            collective_id=0, has_side_effects=True, vmem_limit_bytes=60 * 1024 * 1024
        ),
    )(sel_a, inv_a.reshape(-1), sel_b, inv_b.reshape(-1), coefficients.reshape(GROUPS, 16, COLS), diagonal, alpha_blocks, beta_blocks)


def solution(mesh):
    in_specs = (
        P("alpha", "beta"),
        P("alpha", "beta"),
        P("alpha", None, None, None),
        P(),
        P("beta", None, None, None),
        P(),
    )
    return jax.shard_map(
        per_device, mesh=mesh, in_specs=in_specs, out_specs=P("alpha", "beta"), check_vma=False
    )
```

```python
import jax
import jax.numpy as jnp
from jax import lax
from jax.experimental import pallas as pl
from jax.experimental.pallas import tpu as pltpu
from jax.sharding import PartitionSpec as P

MESH = pl.DeviceIdType.MESH
BLK = 128
SLOTS = 14
RA = 4
RB = 8
CAP_A = 2
CAP_B = 4
ROWS = RA * BLK
COLS = RB * BLK
GROUPS = ROWS // 16
PER = BLK // 16

PIECES = {"n0": (0, 9), "n1": (9, 9), "f0": (18, 7), "f1": (25, 7)}
N_PIECES = ("n0", "n1")
PARTS = ((0, 18), (18, 14))
F_PIECES = ("f0", "f1")
NSEM = 96
COMPUTE = True

INV_A = 0
INV_B = 8
SEL_A = 40
SEL_B = 56
TABLE = 88


def body(la_hbm, lb_hbm, c_hbm, diag_hbm, ab_hbm, bb_hbm, out_hbm, *scratch):
    it = iter(scratch)
    own, own_cb = next(it), next(it)
    gathered = {}
    for dx in range(2):
        for dz in range(4):
            for dc in range(2):
                if (dx, dz, dc) != (0, 0, 0):
                    gathered[dx, dz, dc] = next(it)
    peer = [next(it), next(it)]
    peer_cb = [next(it), next(it)]
    message = {(q, dy): next(it) for q in range(2) for dy in (1, 2, 3)}
    staged = {(q, dy): next(it) for q in range(2) for dy in (1, 2, 3)}
    la, lb, lists_a, lists_b, table, tab, ablk, bblk, diag, acc, out, wa, wb, xa, xb = (next(it) for _ in range(15))
    send_sems, recv_sems, local_sems = it

    ia, ib = lax.axis_index("alpha"), lax.axis_index("beta")
    x_lo, z, core = ia // 8, (ia // 2) % 4, ia % 2
    x_hi, y = ib // 4, ib % 4

    def alpha_at(dx, dz, dc):
        return ((x_lo + dx) % 2) * 8 + ((z + dz) % 4) * 2 + (core + dc) % 2

    def beta_at(dxh, dy):
        return ((x_hi + dxh) % 2) * 4 + (y + dy) % 4

    target = {
        "s": (alpha_at(0, 0, 1), ib),
        "xi": (alpha_at(1, 0, 0), ib),
        "xo": (alpha_at(1, 0, 0), beta_at(1, 0)),
        "z1": (alpha_at(0, 1, 0), ib),
        "z3": (alpha_at(0, 3, 0), ib),
        "y1": (ia, beta_at(0, 1)),
        "y3": (ia, beta_at(0, 3)),
        "y2": (ia, beta_at(0, 2)),
    }
    started = []

    def send(link, src, dst):
        n = len(started)
        copy = pltpu.make_async_remote_copy(
            src_ref=src,
            dst_ref=dst,
            send_sem=send_sems.at[n],
            recv_sem=recv_sems.at[n],
            device_id=target[link],
            device_id_type=MESH,
        )
        copy.start()
        started.append(copy)
        return copy

    def part(ref, piece):
        first, size = PIECES[piece]
        return ref.at[pl.ds(first, size)]

    def local(n, src, dst):
        copy = pltpu.make_async_copy(src, dst, local_sems.at[n])
        copy.start()
        return copy

    load_la = local(0, la_hbm, la)
    load_lb = local(1, lb_hbm, lb)
    load_own = local(2, c_hbm, own)
    barrier = pltpu.get_barrier_semaphore()
    for link in target:
        pl.semaphore_signal(barrier, inc=1, device_id=target[link], device_id_type=MESH)
    load_b = local(3, bb_hbm, bblk.at[:, pl.ds(0, SLOTS)])
    load_d = local(4, diag_hbm, diag)
    load_a = local(5, ab_hbm, ablk.at[:, pl.ds(0, SLOTS)])
    pl.semaphore_wait(barrier, len(target))

    xi, zn, zf, zs, sib = {}, {}, {}, {}, {}
    for p in PIECES:
        xi[p] = send("xi", part(c_hbm, p), part(gathered[1, 0, 0], p))
    zo = {}
    for p in F_PIECES:
        for dz in (1, 3):
            zo[dz, p] = send(f"z{dz}", part(c_hbm, p), part(gathered[0, dz, 0], p))
    for p in N_PIECES:
        for dz in (1, 3):
            zo[dz, p] = send(f"z{dz}", part(c_hbm, p), part(gathered[0, dz, 0], p))
    sib[0, 0] = [send("s", c_hbm, gathered[0, 0, 1])]

    def to_sibling(dx, dz, p):
        copy = send("s", part(gathered[dx, dz, 0], p), part(gathered[dx, dz, 1], p))
        sib.setdefault((dx, dz), []).append(copy)

    lane = lax.broadcasted_iota(jnp.int32, (8, BLK), 1)

    def slots_of(lists):
        inv = jnp.full((8, BLK), SLOTS, jnp.int32)
        for k in range(SLOTS):
            inv = jnp.where(lists[:, k : k + 1] == lane, k, inv)
        return inv

    def picks_of(needed, per, cap, first_row):
        place = lane % per
        shifts = [1 << i for i in range(per.bit_length() - 1)]
        rank = needed
        for shift in shifts:
            rank = rank + jnp.where(place >= shift, pltpu.roll(rank, shift, 1), 0)
        rank = rank - needed
        for s in range(cap):
            pick = jnp.where((needed > 0) & (rank == s), lane, BLK - 1)
            for shift in shifts:
                moved = pltpu.roll(pick, BLK - shift, 1)
                pick = jnp.minimum(pick, jnp.where(place + shift < per, moved, BLK - 1))
            table[first_row + 8 * s : first_row + 8 * s + 8, :] = pick

    load_la.wait()
    load_lb.wait()
    lists_a[...] = la[...].T
    lists_b[...] = lb[...].T
    inv = slots_of(lists_a[pl.ds(pl.multiple_of((ia // 2) * 8, 8), 8), :])
    table[INV_A : INV_A + 8, :] = inv
    row = lax.broadcasted_iota(jnp.int32, (8, BLK), 0)
    mine = (row // RA == core) & (inv < SLOTS)
    needed = jnp.broadcast_to(jnp.max(jnp.where(mine, 1, 0), axis=0, keepdims=True), (8, BLK))
    picks_of(needed, RA, CAP_A, SEL_A)
    needed = jnp.zeros((8, BLK), jnp.int32)
    for d in range(4):
        inv = slots_of(lists_b[pl.ds(pl.multiple_of(x_hi * 32 + d * 8, 8), 8), :])
        table[INV_B + 8 * d : INV_B + 8 * d + 8, :] = inv
        used = jnp.max(jnp.where(inv < SLOTS, 1, 0), axis=0, keepdims=True)
        needed = jnp.where(row == d, used, needed)
    picks_of(needed, RB, CAP_B, SEL_B)

    def by_column(src, dst, groups):
        def group(t, carry):
            for j in range(RB):
                dst[j, pl.ds(pl.multiple_of(t * 16, 16), 16), :] = src[t, :, j * BLK : (j + 1) * BLK]
            return carry

        lax.fori_loop(0, groups, group, 0)

    load_own.wait()
    by_column(own, own_cb, GROUPS)
    for r in range(RA):
        ablk[r, SLOTS] = jnp.zeros((BLK, BLK), jnp.bfloat16)
    for r in range(RB):
        bblk[r, SLOTS] = jnp.zeros((BLK, BLK), jnp.bfloat16)
    load_tab = local(6, table, tab)
    load_tab.wait()

    def pick_b(d, q, s):
        return tab[SEL_B + 8 * s + (y + d) % 4, beta_at(q, 0) * RB] % RB

    sent_b = {}

    def stage_own():
        for dy in (2, 1, 3):
            for s in range(CAP_B):
                staged[0, dy][s] = own_cb[pick_b(dy, 0, s)]

    def send_own():
        for dy in (2, 1, 3):
            sent_b[0, dy] = [send(f"y{dy}", staged[0, dy], message[0, dy])]

    def stage_peer(h):
        for dy in (2, 1, 3):
            for s in range(CAP_B):
                staged[1, dy][s, pl.ds(PARTS[h][0] * 16, PARTS[h][1] * 16), :] = peer_cb[h][pick_b(dy, 1, s)]

    def send_peer(h):
        for dy in (2, 1, 3):
            at = (slice(None), pl.ds(PARTS[h][0] * 16, PARTS[h][1] * 16))
            copy = send(f"y{dy}", staged[1, dy].at[at], message[1, dy].at[at])
            sent_b.setdefault((1, dy), []).append(copy)

    def alpha_weights(dx, dz):
        for dc in range(2):
            owner = alpha_at(dx, 4 - dz, dc)
            for s in range(CAP_A):
                column = (dc * CAP_A + s) * BLK
                pick = tab[SEL_A + 8 * s, owner * RA]
                for r in range(RA):
                    wa[r * BLK : (r + 1) * BLK, column : column + BLK] = ablk[r, tab[INV_A + core * RA + r, pick]]

    def alpha_inputs(dx, dz):
        for dc in range(2):
            owner = alpha_at(dx, 4 - dz, dc)
            source = own if (dx, dz, dc) == (0, 0, 0) else gathered[dx, dz, dc]
            for s in range(CAP_A):
                first = (tab[SEL_A + 8 * s, owner * RA] % RA) * PER
                for t in range(PER):
                    at = (dc * CAP_A + s) * BLK + t * 16
                    xa[at : at + 16, :] = source[first + t]

    def tiles(one):
        def tile(n, carry):
            one(pl.ds(pl.multiple_of(n * 256, 256), 256))
            return carry

        lax.fori_loop(0, COLS // 256, tile, 0)

    def alpha_dot(cols):
        return jnp.dot(wa[...], xa[:, cols], preferred_element_type=jnp.float32)

    def add_alpha(cols):
        acc[:, cols] += alpha_dot(cols)

    def add_beta(cols):
        acc[:, cols] += lax.dot_general(
            xb[...], wb[cols, :], (((1,), (1,)), ((), ())), preferred_element_type=jnp.float32
        )

    def alpha_chip(dx, dz):
        if not COMPUTE:
            return
        alpha_weights(dx, dz)
        alpha_inputs(dx, dz)
        tiles(add_alpha)

    def beta_owner(q, dy):
        if not COMPUTE:
            return
        owner = beta_at(q, 4 - dy)
        for s in range(CAP_B):
            pick = tab[SEL_B + 8 * s + y, owner * RB]
            for r in range(RB):
                wb[r * BLK : (r + 1) * BLK, s * BLK : (s + 1) * BLK] = bblk[r, tab[INV_B + y * RB + r, pick]]
            column = slice(s * BLK, (s + 1) * BLK)
            if dy:
                xb[:, column] = message[q, dy][s]
            elif q:
                for h in range(2):
                    xb[pl.ds(PARTS[h][0] * 16, PARTS[h][1] * 16), column] = peer_cb[h][pick % RB]
            else:
                xb[:, column] = own_cb[pick % RB]
        tiles(add_beta)

    def arrived(copies):
        for copy in copies:
            copy.wait_recv()

    stage_own()
    load_d.wait()

    def init(n, carry):
        at = pl.ds(pl.multiple_of(n * 64, 64), 64)
        acc[at, :] = diag[at, :] * own[pl.ds(n * 4, 4)].astype(jnp.float32).reshape(64, COLS)
        return carry

    lax.fori_loop(0, ROWS // 64, init, 0)
    send_own()
    load_b.wait()
    load_a.wait()
    beta_owner(0, 0)
    arrived(sib[0, 0])
    alpha_chip(0, 0)

    xo = {}

    def over_x(p):
        h = 0 if p in N_PIECES else 1
        first, size = PIECES[p]
        xi[p].wait_recv()
        xo[p] = send("xo", part(gathered[1, 0, 0], p), peer[h].at[pl.ds(first - PARTS[h][0], size)])
        to_sibling(1, 0, p)

    def from_z(copies, dx, dz, pieces):
        for p in pieces:
            copies[dz, p].wait_recv()
            to_sibling(dx, dz, p)

    zx = {}

    def relay(copies, dx, p):
        dz = 1 if p in ("n0", "f0") else 3
        copies[2, p] = send(f"z{dz}", part(gathered[dx, dz, 0], p), part(gathered[dx, 2, 0], p))

    def near_z(copies, dx, p):
        copies[1, p].wait_recv()
        copies[3, p].wait_recv()
        relay(copies, dx, p)
        to_sibling(dx, 1, p)
        to_sibling(dx, 3, p)

    def x_after_z(dz, pieces):
        for p in pieces:
            zx[dz, p] = send("xi", part(gathered[0, dz, 0], p), part(gathered[1, dz, 0], p))

    near_z(zo, 0, "f0")
    over_x("n0")
    near_z(zo, 0, "f1")
    x_after_z(1, F_PIECES)
    x_after_z(3, F_PIECES)
    over_x("n1")
    for p in N_PIECES:
        for dz in (1, 3):
            zx[dz, p] = send(f"z{dz}", part(gathered[1, 0, 0], p), part(gathered[1, dz, 0], p))
    arrived(sent_b[0, 2])
    beta_owner(0, 2)
    near_z(zo, 0, "n0")
    over_x("f0")
    arrived([xo["n0"], xo["n1"]])
    by_column(peer[0], peer_cb[0], PARTS[0][1])
    stage_peer(0)
    near_z(zo, 0, "n1")
    over_x("f1")
    send_peer(0)
    arrived(sent_b[0, 1])
    beta_owner(0, 1)
    arrived(sent_b[0, 3])
    beta_owner(0, 3)
    from_z(zo, 0, 2, F_PIECES)
    x_after_z(2, F_PIECES)
    arrived([xo["f0"], xo["f1"]])
    by_column(peer[1], peer_cb[1], PARTS[1][1])
    stage_peer(1)
    arrived(sib[1, 0])
    alpha_chip(1, 0)
    send_peer(1)
    near_z(zx, 1, "n0")
    arrived(sib[0, 1])
    alpha_chip(0, 1)
    beta_owner(1, 0)
    arrived(sib[0, 3])
    alpha_chip(0, 3)
    near_z(zx, 1, "n1")
    from_z(zx, 1, 1, F_PIECES)
    arrived(sib[1, 1])
    alpha_chip(1, 1)
    arrived(sent_b[1, 2])
    beta_owner(1, 2)
    from_z(zx, 1, 3, F_PIECES)
    arrived(sib[1, 3])
    alpha_chip(1, 3)
    arrived(sent_b[1, 1])
    beta_owner(1, 1)
    arrived(sent_b[1, 3])
    beta_owner(1, 3)
    from_z(zo, 0, 2, N_PIECES)
    arrived(sib[0, 2])
    alpha_chip(0, 2)
    alpha_weights(1, 2)
    from_z(zx, 1, 2, F_PIECES)
    from_z(zx, 1, 2, N_PIECES)
    arrived(sib[1, 2])
    alpha_inputs(1, 2)

    def last(n, carry):
        cols = pl.ds(pl.multiple_of(n * 256, 256), 256)
        out[:, cols] = (acc[:, cols] + alpha_dot(cols)).astype(jnp.bfloat16)
        return carry

    lax.fori_loop(0, COLS // 256, last, 0)
    store = local(7, out, out_hbm)
    for copy in started:
        copy.wait_send()
    store.wait()
    assert len(started) <= NSEM, len(started)


def per_device(coefficients, diagonal, alpha_blocks, alpha_lists, beta_blocks, beta_lists):
    grouped = pltpu.VMEM((GROUPS, 16, COLS), jnp.bfloat16)
    by_block = pltpu.VMEM((RB, ROWS, BLK), jnp.bfloat16)
    slots = pltpu.VMEM((CAP_B, ROWS, BLK), jnp.bfloat16)
    scratch = [grouped, by_block] + [grouped] * 15 + [pltpu.VMEM((n, 16, COLS), jnp.bfloat16) for _, n in PARTS]
    scratch += [pltpu.VMEM((RB, n * 16, BLK), jnp.bfloat16) for _, n in PARTS] + [slots] * 12
    scratch += [
        pltpu.VMEM((SLOTS, 64), jnp.int32),
        pltpu.VMEM((SLOTS, 64), jnp.int32),
        pltpu.VMEM((64, SLOTS), jnp.int32),
        pltpu.VMEM((64, SLOTS), jnp.int32),
        pltpu.VMEM((TABLE, BLK), jnp.int32),
        pltpu.SMEM((TABLE, BLK), jnp.int32),
        pltpu.VMEM((RA, SLOTS + 1, BLK, BLK), jnp.bfloat16),
        pltpu.VMEM((RB, SLOTS + 1, BLK, BLK), jnp.bfloat16),
        pltpu.VMEM((ROWS, COLS), jnp.float32),
        pltpu.VMEM((ROWS, COLS), jnp.float32),
        pltpu.VMEM((ROWS, COLS), jnp.bfloat16),
        pltpu.VMEM((ROWS, 4 * BLK), jnp.bfloat16),
        pltpu.VMEM((COLS, 4 * BLK), jnp.bfloat16),
        pltpu.VMEM((4 * BLK, COLS), jnp.bfloat16),
        pltpu.VMEM((ROWS, 4 * BLK), jnp.bfloat16),
        pltpu.SemaphoreType.DMA((NSEM,)),
        pltpu.SemaphoreType.DMA((NSEM,)),
        pltpu.SemaphoreType.DMA((8,)),
    ]
    return pl.pallas_call(
        body,
        out_shape=jax.ShapeDtypeStruct((ROWS, COLS), jnp.bfloat16),
        in_specs=[pl.BlockSpec(memory_space=pl.ANY)] * 6,
        out_specs=pl.BlockSpec(memory_space=pl.ANY),
        scratch_shapes=scratch,
        compiler_params=pltpu.CompilerParams(
            collective_id=0, has_side_effects=True, vmem_limit_bytes=60 * 1024 * 1024
        ),
    )(
        alpha_lists.T,
        beta_lists.T,
        coefficients.reshape(GROUPS, 16, COLS),
        diagonal,
        alpha_blocks,
        beta_blocks,
    )


def solution(mesh):
    in_specs = (
        P("alpha", "beta"),
        P("alpha", "beta"),
        P("alpha", None, None, None),
        P(),
        P("beta", None, None, None),
        P(),
    )
    return jax.shard_map(
        per_device, mesh=mesh, in_specs=in_specs, out_specs=P("alpha", "beta"), check_vma=False
    )
```

```python
import jax
import jax.numpy as jnp
from jax import lax
from jax.experimental import pallas as pl
from jax.experimental.pallas import tpu as pltpu
from jax.sharding import PartitionSpec as P

MESH = pl.DeviceIdType.MESH
BLK = 128
SLOTS = 14
RA = 4
RB = 8
CAP_A = 2
CAP_B = 4
ROWS = RA * BLK
COLS = RB * BLK
GROUPS = ROWS // 16
PER = BLK // 16

PIECES = {"n0": (0, 9), "n1": (9, 9), "f0": (18, 7), "f1": (25, 7)}
N_PIECES = ("n0", "n1")
PARTS = ((0, 18), (18, 14))
F_PIECES = ("f0", "f1")
NSEM = 96
COMPUTE = True

INV_A = 0
INV_B = 8
SEL_A = 40
SEL_B = 56
TABLE = 88


def body(la_hbm, lb_hbm, c_hbm, diag_hbm, ab_hbm, bb_hbm, out_ref, *scratch):
    it = iter(scratch)
    own, own_cb = next(it), next(it)
    gathered = {}
    for dx in range(2):
        for dz in range(4):
            for dc in range(2):
                if (dx, dz, dc) != (0, 0, 0):
                    gathered[dx, dz, dc] = next(it)
    peer = [next(it), next(it)]
    peer_cb = [next(it), next(it)]
    message = {(q, dy): next(it) for q in range(2) for dy in (1, 2, 3)}
    staged = {(q, dy): next(it) for q in range(2) for dy in (1, 2, 3)}
    la, lb, lists_a, lists_b, table, tab, ablk, bblk, diag, acc, wa, wb, xa, xb = (next(it) for _ in range(14))
    send_sems, recv_sems, local_sems = it

    ia, ib = lax.axis_index("alpha"), lax.axis_index("beta")
    x_lo, z, core = ia // 8, (ia // 2) % 4, ia % 2
    x_hi, y = ib // 4, ib % 4

    def alpha_at(dx, dz, dc):
        return ((x_lo + dx) % 2) * 8 + ((z + dz) % 4) * 2 + (core + dc) % 2

    def beta_at(dxh, dy):
        return ((x_hi + dxh) % 2) * 4 + (y + dy) % 4

    target = {
        "s": (alpha_at(0, 0, 1), ib),
        "xi": (alpha_at(1, 0, 0), ib),
        "xo": (alpha_at(1, 0, 0), beta_at(1, 0)),
        "z1": (alpha_at(0, 1, 0), ib),
        "z3": (alpha_at(0, 3, 0), ib),
        "y1": (ia, beta_at(0, 1)),
        "y3": (ia, beta_at(0, 3)),
        "y2": (ia, beta_at(0, 2)),
    }
    started = []

    def send(link, src, dst):
        n = len(started)
        copy = pltpu.make_async_remote_copy(
            src_ref=src,
            dst_ref=dst,
            send_sem=send_sems.at[n],
            recv_sem=recv_sems.at[n],
            device_id=target[link],
            device_id_type=MESH,
        )
        copy.start()
        started.append(copy)
        return copy

    def part(ref, piece):
        first, size = PIECES[piece]
        return ref.at[pl.ds(first, size)]

    def local(n, src, dst):
        copy = pltpu.make_async_copy(src, dst, local_sems.at[n])
        copy.start()
        return copy

    load_la = local(0, la_hbm, la)
    load_lb = local(1, lb_hbm, lb)
    load_own = local(2, c_hbm, own)
    barrier = pltpu.get_barrier_semaphore()
    for link in target:
        pl.semaphore_signal(barrier, inc=1, device_id=target[link], device_id_type=MESH)
    load_b = local(3, bb_hbm, bblk.at[:, pl.ds(0, SLOTS)])
    load_d = local(4, diag_hbm, diag)
    load_a = local(5, ab_hbm, ablk.at[:, pl.ds(0, SLOTS)])
    pl.semaphore_wait(barrier, len(target))

    xi, zn, zf, zs, sib = {}, {}, {}, {}, {}
    for p in PIECES:
        xi[p] = send("xi", part(c_hbm, p), part(gathered[1, 0, 0], p))
    zo = {}
    for p in F_PIECES:
        for dz in (1, 3):
            zo[dz, p] = send(f"z{dz}", part(c_hbm, p), part(gathered[0, dz, 0], p))
    for p in N_PIECES:
        for dz in (1, 3):
            zo[dz, p] = send(f"z{dz}", part(c_hbm, p), part(gathered[0, dz, 0], p))
    sib[0, 0] = [send("s", c_hbm, gathered[0, 0, 1])]

    def to_sibling(dx, dz, p):
        copy = send("s", part(gathered[dx, dz, 0], p), part(gathered[dx, dz, 1], p))
        sib.setdefault((dx, dz), []).append(copy)

    lane = lax.broadcasted_iota(jnp.int32, (8, BLK), 1)

    def slots_of(lists):
        inv = jnp.full((8, BLK), SLOTS, jnp.int32)
        for k in range(SLOTS):
            inv = jnp.where(lists[:, k : k + 1] == lane, k, inv)
        return inv

    def picks_of(needed, per, cap, first_row):
        place = lane % per
        shifts = [1 << i for i in range(per.bit_length() - 1)]
        rank = needed
        for shift in shifts:
            rank = rank + jnp.where(place >= shift, pltpu.roll(rank, shift, 1), 0)
        rank = rank - needed
        for s in range(cap):
            pick = jnp.where((needed > 0) & (rank == s), lane, BLK - 1)
            for shift in shifts:
                moved = pltpu.roll(pick, BLK - shift, 1)
                pick = jnp.minimum(pick, jnp.where(place + shift < per, moved, BLK - 1))
            table[first_row + 8 * s : first_row + 8 * s + 8, :] = pick

    load_la.wait()
    load_lb.wait()
    lists_a[...] = la[...].T
    lists_b[...] = lb[...].T
    inv = slots_of(lists_a[pl.ds(pl.multiple_of((ia // 2) * 8, 8), 8), :])
    table[INV_A : INV_A + 8, :] = inv
    row = lax.broadcasted_iota(jnp.int32, (8, BLK), 0)
    mine = (row // RA == core) & (inv < SLOTS)
    needed = jnp.broadcast_to(jnp.max(jnp.where(mine, 1, 0), axis=0, keepdims=True), (8, BLK))
    picks_of(needed, RA, CAP_A, SEL_A)
    needed = jnp.zeros((8, BLK), jnp.int32)
    for d in range(4):
        inv = slots_of(lists_b[pl.ds(pl.multiple_of(x_hi * 32 + d * 8, 8), 8), :])
        table[INV_B + 8 * d : INV_B + 8 * d + 8, :] = inv
        used = jnp.max(jnp.where(inv < SLOTS, 1, 0), axis=0, keepdims=True)
        needed = jnp.where(row == d, used, needed)
    picks_of(needed, RB, CAP_B, SEL_B)

    def by_column(src, dst, groups):
        def group(t, carry):
            for j in range(RB):
                dst[j, pl.ds(pl.multiple_of(t * 16, 16), 16), :] = src[t, :, j * BLK : (j + 1) * BLK]
            return carry

        lax.fori_loop(0, groups, group, 0)

    load_own.wait()
    by_column(own, own_cb, GROUPS)
    load_tab = local(6, table, tab)
    load_tab.wait()

    def pick_b(d, q, s):
        return tab[SEL_B + 8 * s + (y + d) % 4, beta_at(q, 0) * RB] % RB

    sent_b = {}

    def stage_own():
        for dy in (2, 1, 3):
            for s in range(CAP_B):
                staged[0, dy][s] = own_cb[pick_b(dy, 0, s)]

    def send_own():
        for dy in (2, 1, 3):
            sent_b[0, dy] = [send(f"y{dy}", staged[0, dy], message[0, dy])]

    def stage_peer(h):
        for dy in (2, 1, 3):
            for s in range(CAP_B):
                staged[1, dy][s, pl.ds(PARTS[h][0] * 16, PARTS[h][1] * 16), :] = peer_cb[h][pick_b(dy, 1, s)]

    def send_peer(h):
        for dy in (2, 1, 3):
            at = (slice(None), pl.ds(PARTS[h][0] * 16, PARTS[h][1] * 16))
            copy = send(f"y{dy}", staged[1, dy].at[at], message[1, dy].at[at])
            sent_b.setdefault((1, dy), []).append(copy)

    def alpha_weights(dx, dz):
        for dc in range(2):
            owner = alpha_at(dx, 4 - dz, dc)
            for s in range(CAP_A):
                column = (dc * CAP_A + s) * BLK
                pick = tab[SEL_A + 8 * s, owner * RA]
                for r in range(RA):
                    wa[r * BLK : (r + 1) * BLK, column : column + BLK] = ablk[r, tab[INV_A + core * RA + r, pick]]

    def alpha_inputs(dx, dz, *lanes):
        for dc in lanes:
            owner = alpha_at(dx, 4 - dz, dc)
            source = own if (dx, dz, dc) == (0, 0, 0) else gathered[dx, dz, dc]
            for s in range(CAP_A):
                first = (tab[SEL_A + 8 * s, owner * RA] % RA) * PER
                for t in range(PER):
                    at = (dc * CAP_A + s) * BLK + t * 16
                    xa[at : at + 16, :] = source[first + t]

    def tiles(one):
        def tile(n, carry):
            one(pl.ds(pl.multiple_of(n * 256, 256), 256))
            return carry

        lax.fori_loop(0, COLS // 256, tile, 0)

    def alpha_dot(cols, *lanes):
        depth = pl.ds(lanes[0] * CAP_A * BLK, len(lanes) * CAP_A * BLK)
        return jnp.dot(wa[:, depth], xa[depth, cols], preferred_element_type=jnp.float32)

    def add_alpha(cols):
        acc[:, cols] += alpha_dot(cols, 0, 1)

    def add_alpha_lane(cols):
        acc[:, cols] += alpha_dot(cols, 0)

    def add_beta(cols):
        acc[:, cols] += lax.dot_general(
            xb[...], wb[cols, :], (((1,), (1,)), ((), ())), preferred_element_type=jnp.float32
        )

    def alpha_chip(dx, dz):
        if not COMPUTE:
            return
        alpha_weights(dx, dz)
        alpha_inputs(dx, dz, 0, 1)
        tiles(add_alpha)

    def beta_owner(q, dy):
        if not COMPUTE:
            return
        owner = beta_at(q, 4 - dy)
        for s in range(CAP_B):
            pick = tab[SEL_B + 8 * s + y, owner * RB]
            for r in range(RB):
                wb[r * BLK : (r + 1) * BLK, s * BLK : (s + 1) * BLK] = bblk[r, tab[INV_B + y * RB + r, pick]]
            column = slice(s * BLK, (s + 1) * BLK)
            if dy:
                xb[:, column] = message[q, dy][s]
            elif q:
                for h in range(2):
                    xb[pl.ds(PARTS[h][0] * 16, PARTS[h][1] * 16), column] = peer_cb[h][pick % RB]
            else:
                xb[:, column] = own_cb[pick % RB]
        tiles(add_beta)

    def arrived(copies):
        for copy in copies:
            copy.wait_recv()

    stage_own()
    for r in range(RA):
        ablk[r, SLOTS] = jnp.zeros((BLK, BLK), jnp.bfloat16)
    for r in range(RB):
        bblk[r, SLOTS] = jnp.zeros((BLK, BLK), jnp.bfloat16)
    send_own()
    load_d.wait()

    def init(n, carry):
        at = pl.ds(pl.multiple_of(n * 64, 64), 64)
        acc[at, :] = diag[at, :] * own[pl.ds(n * 4, 4)].astype(jnp.float32).reshape(64, COLS)
        return carry

    lax.fori_loop(0, ROWS // 64, init, 0)
    load_b.wait()
    load_a.wait()
    beta_owner(0, 0)
    arrived(sib[0, 0])
    alpha_chip(0, 0)

    xo = {}

    def over_x(p):
        h = 0 if p in N_PIECES else 1
        first, size = PIECES[p]
        xi[p].wait_recv()
        xo[p] = send("xo", part(gathered[1, 0, 0], p), peer[h].at[pl.ds(first - PARTS[h][0], size)])
        to_sibling(1, 0, p)

    def from_z(copies, dx, dz, pieces):
        for p in pieces:
            copies[dz, p].wait_recv()
            to_sibling(dx, dz, p)

    zx = {}

    def relay(copies, dx, p):
        dz = 1 if p in ("n0", "f0") else 3
        copies[2, p] = send(f"z{dz}", part(gathered[dx, dz, 0], p), part(gathered[dx, 2, 0], p))

    def near_z(copies, dx, p):
        copies[1, p].wait_recv()
        copies[3, p].wait_recv()
        relay(copies, dx, p)
        to_sibling(dx, 1, p)
        to_sibling(dx, 3, p)

    def x_after_z(dz, pieces):
        for p in pieces:
            zx[dz, p] = send("xi", part(gathered[0, dz, 0], p), part(gathered[1, dz, 0], p))

    near_z(zo, 0, "f0")
    over_x("n0")
    near_z(zo, 0, "f1")
    x_after_z(1, F_PIECES)
    x_after_z(3, F_PIECES)
    over_x("n1")
    for p in N_PIECES:
        for dz in (1, 3):
            zx[dz, p] = send(f"z{dz}", part(gathered[1, 0, 0], p), part(gathered[1, dz, 0], p))
    arrived(sent_b[0, 2])
    beta_owner(0, 2)
    near_z(zo, 0, "n0")
    over_x("f0")
    arrived([xo["n0"], xo["n1"]])
    by_column(peer[0], peer_cb[0], PARTS[0][1])
    stage_peer(0)
    near_z(zo, 0, "n1")
    over_x("f1")
    send_peer(0)
    arrived(sent_b[0, 1])
    beta_owner(0, 1)
    arrived(sent_b[0, 3])
    beta_owner(0, 3)
    from_z(zo, 0, 2, F_PIECES)
    x_after_z(2, F_PIECES)
    arrived([xo["f0"], xo["f1"]])
    by_column(peer[1], peer_cb[1], PARTS[1][1])
    stage_peer(1)
    from_z(zx, 1, 1, F_PIECES)
    arrived(sib[1, 0])
    alpha_chip(1, 0)
    send_peer(1)
    near_z(zx, 1, "n0")
    arrived(sib[0, 1])
    alpha_chip(0, 1)
    beta_owner(1, 0)
    arrived(sib[0, 3])
    alpha_chip(0, 3)
    near_z(zx, 1, "n1")
    arrived(sib[1, 1])
    alpha_chip(1, 1)
    from_z(zx, 1, 3, F_PIECES)
    arrived(sent_b[1, 2])
    beta_owner(1, 2)
    arrived(sib[1, 3])
    alpha_chip(1, 3)
    from_z(zo, 0, 2, N_PIECES)
    from_z(zx, 1, 2, ("f0",))
    arrived(sent_b[1, 1])
    beta_owner(1, 1)
    arrived(sent_b[1, 3])
    beta_owner(1, 3)
    arrived(sib[0, 2])
    alpha_chip(0, 2)
    alpha_weights(1, 2)
    from_z(zx, 1, 2, ("f1",) + N_PIECES)
    alpha_inputs(1, 2, 0)
    tiles(add_alpha_lane)
    arrived(sib[1, 2])
    alpha_inputs(1, 2, 1)

    def last(n, carry):
        cols = pl.ds(pl.multiple_of(n * 256, 256), 256)
        out_ref[:, cols] = (acc[:, cols] + alpha_dot(cols, 1)).astype(jnp.bfloat16)
        return carry

    lax.fori_loop(0, COLS // 256, last, 0)
    for copy in started:
        copy.wait_send()
    assert len(started) <= NSEM, len(started)


def per_device(coefficients, diagonal, alpha_blocks, alpha_lists, beta_blocks, beta_lists):
    grouped = pltpu.VMEM((GROUPS, 16, COLS), jnp.bfloat16)
    by_block = pltpu.VMEM((RB, ROWS, BLK), jnp.bfloat16)
    slots = pltpu.VMEM((CAP_B, ROWS, BLK), jnp.bfloat16)
    scratch = [grouped, by_block] + [grouped] * 15 + [pltpu.VMEM((n, 16, COLS), jnp.bfloat16) for _, n in PARTS]
    scratch += [pltpu.VMEM((RB, n * 16, BLK), jnp.bfloat16) for _, n in PARTS] + [slots] * 12
    scratch += [
        pltpu.VMEM((SLOTS, 64), jnp.int32),
        pltpu.VMEM((SLOTS, 64), jnp.int32),
        pltpu.VMEM((64, SLOTS), jnp.int32),
        pltpu.VMEM((64, SLOTS), jnp.int32),
        pltpu.VMEM((TABLE, BLK), jnp.int32),
        pltpu.SMEM((TABLE, BLK), jnp.int32),
        pltpu.VMEM((RA, SLOTS + 1, BLK, BLK), jnp.bfloat16),
        pltpu.VMEM((RB, SLOTS + 1, BLK, BLK), jnp.bfloat16),
        pltpu.VMEM((ROWS, COLS), jnp.float32),
        pltpu.VMEM((ROWS, COLS), jnp.float32),
        pltpu.VMEM((ROWS, 4 * BLK), jnp.bfloat16),
        pltpu.VMEM((COLS, 4 * BLK), jnp.bfloat16),
        pltpu.VMEM((4 * BLK, COLS), jnp.bfloat16),
        pltpu.VMEM((ROWS, 4 * BLK), jnp.bfloat16),
        pltpu.SemaphoreType.DMA((NSEM,)),
        pltpu.SemaphoreType.DMA((NSEM,)),
        pltpu.SemaphoreType.DMA((7,)),
    ]
    return pl.pallas_call(
        body,
        out_shape=pltpu.VMEM((ROWS, COLS), jnp.bfloat16),
        in_specs=[pl.BlockSpec(memory_space=pl.ANY)] * 6,
        out_specs=pl.BlockSpec(memory_space=pltpu.VMEM),
        scratch_shapes=scratch,
        compiler_params=pltpu.CompilerParams(
            collective_id=0, has_side_effects=True, vmem_limit_bytes=60 * 1024 * 1024
        ),
    )(
        alpha_lists.T,
        beta_lists.T,
        coefficients.reshape(GROUPS, 16, COLS),
        diagonal,
        alpha_blocks,
        beta_blocks,
    )


def solution(mesh):
    in_specs = (
        P("alpha", "beta"),
        P("alpha", "beta"),
        P("alpha", None, None, None),
        P(),
        P("beta", None, None, None),
        P(),
    )
    return jax.shard_map(
        per_device, mesh=mesh, in_specs=in_specs, out_specs=P("alpha", "beta"), check_vma=False
    )
```

```python
import jax
import jax.numpy as jnp
from jax import lax
from jax.experimental import pallas as pl
from jax.experimental.pallas import tpu as pltpu
from jax.sharding import PartitionSpec as P

MESH = pl.DeviceIdType.MESH
BLK = 128
SLOTS = 14
RA = 4
RB = 8
CAP_A = 2
CAP_B = 4
ROWS = RA * BLK
COLS = RB * BLK
GROUPS = ROWS // 16
PER = BLK // 16

PIECES = {
    "n": (0, 17),
    "n0": (0, 8),
    "n1": (8, 9),
    "n0a": (0, 5),
    "n0b": (5, 3),
    "n1a": (8, 6),
    "n1b": (14, 3),
    "f": (17, 15),
    "f0": (17, 8),
    "f1": (25, 7),
    "fa": (17, 11),
    "fb": (28, 4),
}
PARTS = (PIECES["n"], PIECES["f"])
NSEM = 96
COMPUTE = True

INV_A = 0
INV_B = 8
SEL_A = 40
SEL_B = 56
TABLE = 88


def body(la_hbm, lb_hbm, c_hbm, diag_hbm, ab_hbm, bb_hbm, out_ref, *scratch):
    it = iter(scratch)
    own, own_cb = next(it), next(it)
    gathered = {}
    for dx in range(2):
        for dz in range(4):
            for dc in range(2):
                if (dx, dz, dc) != (0, 0, 0):
                    gathered[dx, dz, dc] = next(it)
    peer = [next(it), next(it)]
    peer_cb = [next(it), next(it)]
    message = {(q, dy): next(it) for q in range(2) for dy in (1, 2, 3)}
    staged = {(q, dy): next(it) for q in range(2) for dy in (1, 2, 3)}
    la, lb, lists_a, lists_b, table, tab, ablk, bblk, diag, acc, wa, wb, xa, xb = (next(it) for _ in range(14))
    send_sems, recv_sems, local_sems = it

    ia, ib = lax.axis_index("alpha"), lax.axis_index("beta")
    x_lo, z, core = ia // 8, (ia // 2) % 4, ia % 2
    x_hi, y = ib // 4, ib % 4

    def alpha_at(dx, dz, dc):
        return ((x_lo + dx) % 2) * 8 + ((z + dz) % 4) * 2 + (core + dc) % 2

    def beta_at(dxh, dy):
        return ((x_hi + dxh) % 2) * 4 + (y + dy) % 4

    target = {
        "s": (alpha_at(0, 0, 1), ib),
        "xi": (alpha_at(1, 0, 0), ib),
        "xo": (alpha_at(1, 0, 0), beta_at(1, 0)),
        "z1": (alpha_at(0, 1, 0), ib),
        "z3": (alpha_at(0, 3, 0), ib),
        "y1": (ia, beta_at(0, 1)),
        "y3": (ia, beta_at(0, 3)),
        "y2": (ia, beta_at(0, 2)),
    }
    started = []

    def send(link, src, dst):
        n = len(started)
        copy = pltpu.make_async_remote_copy(
            src_ref=src,
            dst_ref=dst,
            send_sem=send_sems.at[n],
            recv_sem=recv_sems.at[n],
            device_id=target[link],
            device_id_type=MESH,
        )
        copy.start()
        started.append(copy)
        return copy

    def part(ref, piece):
        first, size = PIECES[piece]
        return ref.at[pl.ds(first, size)]

    def local(n, src, dst):
        copy = pltpu.make_async_copy(src, dst, local_sems.at[n])
        copy.start()
        return copy

    load_la = local(0, la_hbm, la)
    load_lb = local(1, lb_hbm, lb)
    load_own = local(2, c_hbm, own)
    barrier = pltpu.get_barrier_semaphore()
    for link in target:
        pl.semaphore_signal(barrier, inc=1, device_id=target[link], device_id_type=MESH)
    load_b = local(3, bb_hbm, bblk.at[:, pl.ds(0, SLOTS)])
    load_d = local(4, diag_hbm, diag)
    load_a = local(5, ab_hbm, ablk.at[:, pl.ds(0, SLOTS)])
    pl.semaphore_wait(barrier, len(target))

    xi, zn, zf, zs, sib = {}, {}, {}, {}, {}
    for p in ("n0", "n1", "f0", "f1"):
        xi[p] = send("xi", part(c_hbm, p), part(gathered[1, 0, 0], p))
    zo = {}
    for p in ("f", "n"):
        for dz in (1, 3):
            zo[dz, p] = send(f"z{dz}", part(c_hbm, p), part(gathered[0, dz, 0], p))
    sib[0, 0] = [send("s", c_hbm, gathered[0, 0, 1])]

    def to_sibling(dx, dz, p):
        copy = send("s", part(gathered[dx, dz, 0], p), part(gathered[dx, dz, 1], p))
        sib.setdefault((dx, dz), []).append(copy)

    lane = lax.broadcasted_iota(jnp.int32, (8, BLK), 1)

    def slots_of(lists):
        inv = jnp.full((8, BLK), SLOTS, jnp.int32)
        for k in range(SLOTS):
            inv = jnp.where(lists[:, k : k + 1] == lane, k, inv)
        return inv

    def picks_of(needed, per, cap, first_row):
        place = lane % per
        shifts = [1 << i for i in range(per.bit_length() - 1)]
        rank = needed
        for shift in shifts:
            rank = rank + jnp.where(place >= shift, pltpu.roll(rank, shift, 1), 0)
        rank = rank - needed
        for s in range(cap):
            pick = jnp.where((needed > 0) & (rank == s), lane, BLK - 1)
            for shift in shifts:
                moved = pltpu.roll(pick, BLK - shift, 1)
                pick = jnp.minimum(pick, jnp.where(place + shift < per, moved, BLK - 1))
            table[first_row + 8 * s : first_row + 8 * s + 8, :] = pick

    load_la.wait()
    load_lb.wait()
    lists_a[...] = la[...].T
    lists_b[...] = lb[...].T
    inv = slots_of(lists_a[pl.ds(pl.multiple_of((ia // 2) * 8, 8), 8), :])
    table[INV_A : INV_A + 8, :] = inv
    row = lax.broadcasted_iota(jnp.int32, (8, BLK), 0)
    mine = (row // RA == core) & (inv < SLOTS)
    needed = jnp.broadcast_to(jnp.max(jnp.where(mine, 1, 0), axis=0, keepdims=True), (8, BLK))
    picks_of(needed, RA, CAP_A, SEL_A)
    needed = jnp.zeros((8, BLK), jnp.int32)
    for d in range(4):
        inv = slots_of(lists_b[pl.ds(pl.multiple_of(x_hi * 32 + d * 8, 8), 8), :])
        table[INV_B + 8 * d : INV_B + 8 * d + 8, :] = inv
        used = jnp.max(jnp.where(inv < SLOTS, 1, 0), axis=0, keepdims=True)
        needed = jnp.where(row == d, used, needed)
    picks_of(needed, RB, CAP_B, SEL_B)

    def by_column(src, dst, groups):
        def group(t, carry):
            for j in range(RB):
                dst[j, pl.ds(pl.multiple_of(t * 16, 16), 16), :] = src[t, :, j * BLK : (j + 1) * BLK]
            return carry

        lax.fori_loop(0, groups, group, 0)

    for r in range(RA):
        ablk[r, SLOTS] = jnp.zeros((BLK, BLK), jnp.bfloat16)
    for r in range(RB):
        bblk[r, SLOTS] = jnp.zeros((BLK, BLK), jnp.bfloat16)
    load_own.wait()
    load_tab = local(6, table, tab)
    by_column(own, own_cb, GROUPS)
    load_tab.wait()

    def pick_b(d, q, s):
        return tab[SEL_B + 8 * s + (y + d) % 4, beta_at(q, 0) * RB] % RB

    sent_b = {}

    def stage_own():
        for dy in (2, 1, 3):
            for s in range(CAP_B):
                staged[0, dy][s] = own_cb[pick_b(dy, 0, s)]

    def send_own():
        for dy in (2, 1, 3):
            sent_b[0, dy] = [send(f"y{dy}", staged[0, dy], message[0, dy])]

    def stage_peer(h):
        for dy in (2, 1, 3):
            for s in range(CAP_B):
                staged[1, dy][s, pl.ds(PARTS[h][0] * 16, PARTS[h][1] * 16), :] = peer_cb[h][pick_b(dy, 1, s)]

    def send_peer(h):
        for dy in (2, 1, 3):
            at = (slice(None), pl.ds(PARTS[h][0] * 16, PARTS[h][1] * 16))
            copy = send(f"y{dy}", staged[1, dy].at[at], message[1, dy].at[at])
            sent_b.setdefault((1, dy), []).append(copy)

    def alpha_weights(dx, dz):
        for dc in range(2):
            owner = alpha_at(dx, 4 - dz, dc)
            for s in range(CAP_A):
                column = (dc * CAP_A + s) * BLK
                pick = tab[SEL_A + 8 * s, owner * RA]
                for r in range(RA):
                    wa[r * BLK : (r + 1) * BLK, column : column + BLK] = ablk[r, tab[INV_A + core * RA + r, pick]]

    def alpha_inputs(dx, dz, *lanes):
        for dc in lanes:
            owner = alpha_at(dx, 4 - dz, dc)
            source = own if (dx, dz, dc) == (0, 0, 0) else gathered[dx, dz, dc]
            for s in range(CAP_A):
                first = (tab[SEL_A + 8 * s, owner * RA] % RA) * PER
                for t in range(PER):
                    at = (dc * CAP_A + s) * BLK + t * 16
                    xa[at : at + 16, :] = source[first + t]

    def tiles(one):
        def tile(n, carry):
            one(pl.ds(pl.multiple_of(n * 256, 256), 256))
            return carry

        lax.fori_loop(0, COLS // 256, tile, 0)

    def alpha_dot(cols, *lanes):
        depth = pl.ds(lanes[0] * CAP_A * BLK, len(lanes) * CAP_A * BLK)
        return jnp.dot(wa[:, depth], xa[depth, cols], preferred_element_type=jnp.float32)

    def add_alpha(cols):
        acc[:, cols] += alpha_dot(cols, 0, 1)

    def add_alpha_lane(cols):
        acc[:, cols] += alpha_dot(cols, 0)

    def add_beta(cols):
        acc[:, cols] += lax.dot_general(
            xb[...], wb[cols, :], (((1,), (1,)), ((), ())), preferred_element_type=jnp.float32
        )

    def alpha_chip(dx, dz):
        if not COMPUTE:
            return
        alpha_weights(dx, dz)
        alpha_inputs(dx, dz, 0, 1)
        tiles(add_alpha)

    def beta_owner(q, dy):
        if not COMPUTE:
            return
        owner = beta_at(q, 4 - dy)
        for s in range(CAP_B):
            pick = tab[SEL_B + 8 * s + y, owner * RB]
            for r in range(RB):
                wb[r * BLK : (r + 1) * BLK, s * BLK : (s + 1) * BLK] = bblk[r, tab[INV_B + y * RB + r, pick]]
            column = slice(s * BLK, (s + 1) * BLK)
            if dy:
                xb[:, column] = message[q, dy][s]
            elif q:
                for h in range(2):
                    xb[pl.ds(PARTS[h][0] * 16, PARTS[h][1] * 16), column] = peer_cb[h][pick % RB]
            else:
                xb[:, column] = own_cb[pick % RB]
        tiles(add_beta)

    def arrived(copies):
        for copy in copies:
            copy.wait_recv()

    stage_own()
    send_own()
    load_d.wait()

    def init(n, carry):
        at = pl.ds(pl.multiple_of(n * 64, 64), 64)
        acc[at, :] = diag[at, :] * own[pl.ds(n * 4, 4)].astype(jnp.float32).reshape(64, COLS)
        return carry

    lax.fori_loop(0, ROWS // 64, init, 0)
    load_b.wait()
    load_a.wait()
    beta_owner(0, 0)
    arrived(sib[0, 0])
    alpha_chip(0, 0)

    xo = {}

    def over_x(p):
        h = int(p in ("f0", "f1"))
        first, size = PIECES[p]
        xi[p].wait_recv()
        xo[p] = send("xo", part(gathered[1, 0, 0], p), peer[h].at[pl.ds(first - PARTS[h][0], size)])

    zx = {}

    def relay(copies, dx, *pieces):
        for p in pieces:
            dz = 1 if p[:2] in ("n0", "f0") else 3
            copies[2, p] = send(f"z{dz}", part(gathered[dx, dz, 0], p), part(gathered[dx, 2, 0], p))

    def near_z(copies, dx, p, *halves):
        for dz in (1, 3):
            copies[dz, p].wait_recv()
        relay(copies, dx, *halves)
        for dz in (1, 3):
            to_sibling(dx, dz, p)

    def after(copies, dx, dz, *pieces):
        for p in pieces:
            copies[dz, p].wait_recv()
            to_sibling(dx, dz, p)

    def x_after_z(dz, *pieces):
        for p in pieces:
            zx[dz, p] = send("xi", part(gathered[0, dz, 0], p), part(gathered[1, dz, 0], p))

    over_x("n0")
    near_z(zo, 0, "f", "f0", "f1")
    x_after_z(1, "f")
    x_after_z(3, "f")
    over_x("n1")
    for dz in (1, 3):
        zx[dz, "n"] = send(f"z{dz}", part(gathered[1, 0, 0], "n"), part(gathered[1, dz, 0], "n"))
    to_sibling(1, 0, "n")
    arrived(sent_b[0, 2])
    beta_owner(0, 2)
    over_x("f0")
    arrived([xo["n0"], xo["n1"]])
    by_column(peer[0], peer_cb[0], PARTS[0][1])
    stage_peer(0)
    send_peer(0)
    near_z(zo, 0, "n", "n0", "n1")
    over_x("f1")
    to_sibling(1, 0, "f")
    arrived(sent_b[0, 1])
    beta_owner(0, 1)
    arrived(sent_b[0, 3])
    beta_owner(0, 3)
    after(zo, 0, 2, "f0", "f1")
    x_after_z(2, "fa", "fb")
    arrived([xo["f0"], xo["f1"]])
    by_column(peer[1], peer_cb[1], PARTS[1][1])
    stage_peer(1)
    after(zx, 1, 1, "f")
    arrived(sib[1, 0])
    send_peer(1)
    alpha_chip(1, 0)
    arrived(sib[0, 1])
    alpha_chip(0, 1)
    beta_owner(1, 0)
    near_z(zx, 1, "n", "n0a", "n0b", "n1a", "n1b")
    arrived(sib[0, 3])
    alpha_chip(0, 3)
    arrived(sib[1, 1])
    alpha_chip(1, 1)
    after(zx, 1, 3, "f")
    arrived(sent_b[1, 2])
    beta_owner(1, 2)
    after(zo, 0, 2, "n0", "n1")
    arrived(sib[1, 3])
    alpha_chip(1, 3)
    arrived(sib[0, 2])
    alpha_chip(0, 2)
    arrived(sent_b[1, 1])
    beta_owner(1, 1)
    after(zx, 1, 2, "n0a", "n1a")
    arrived(sent_b[1, 3])
    beta_owner(1, 3)
    alpha_weights(1, 2)
    after(zx, 1, 2, "n0b", "fa", "n1b", "fb")
    alpha_inputs(1, 2, 0)
    tiles(add_alpha_lane)
    arrived(sib[1, 2])
    alpha_inputs(1, 2, 1)

    def last(n, carry):
        cols = pl.ds(pl.multiple_of(n * 256, 256), 256)
        out_ref[:, cols] = (acc[:, cols] + alpha_dot(cols, 1)).astype(jnp.bfloat16)
        return carry

    lax.fori_loop(0, COLS // 256, last, 0)
    for copy in started:
        copy.wait_send()
    assert len(started) <= NSEM, len(started)


def per_device(coefficients, diagonal, alpha_blocks, alpha_lists, beta_blocks, beta_lists):
    grouped = pltpu.VMEM((GROUPS, 16, COLS), jnp.bfloat16)
    by_block = pltpu.VMEM((RB, ROWS, BLK), jnp.bfloat16)
    slots = pltpu.VMEM((CAP_B, ROWS, BLK), jnp.bfloat16)
    scratch = [grouped, by_block] + [grouped] * 15 + [pltpu.VMEM((n, 16, COLS), jnp.bfloat16) for _, n in PARTS]
    scratch += [pltpu.VMEM((RB, n * 16, BLK), jnp.bfloat16) for _, n in PARTS] + [slots] * 12
    scratch += [
        pltpu.VMEM((SLOTS, 64), jnp.int32),
        pltpu.VMEM((SLOTS, 64), jnp.int32),
        pltpu.VMEM((64, SLOTS), jnp.int32),
        pltpu.VMEM((64, SLOTS), jnp.int32),
        pltpu.VMEM((TABLE, BLK), jnp.int32),
        pltpu.SMEM((TABLE, BLK), jnp.int32),
        pltpu.VMEM((RA, SLOTS + 1, BLK, BLK), jnp.bfloat16),
        pltpu.VMEM((RB, SLOTS + 1, BLK, BLK), jnp.bfloat16),
        pltpu.VMEM((ROWS, COLS), jnp.float32),
        pltpu.VMEM((ROWS, COLS), jnp.float32),
        pltpu.VMEM((ROWS, 4 * BLK), jnp.bfloat16),
        pltpu.VMEM((COLS, 4 * BLK), jnp.bfloat16),
        pltpu.VMEM((4 * BLK, COLS), jnp.bfloat16),
        pltpu.VMEM((ROWS, 4 * BLK), jnp.bfloat16),
        pltpu.SemaphoreType.DMA((NSEM,)),
        pltpu.SemaphoreType.DMA((NSEM,)),
        pltpu.SemaphoreType.DMA((7,)),
    ]
    return pl.pallas_call(
        body,
        out_shape=pltpu.VMEM((ROWS, COLS), jnp.bfloat16),
        in_specs=[pl.BlockSpec(memory_space=pl.ANY)] * 6,
        out_specs=pl.BlockSpec(memory_space=pltpu.VMEM),
        scratch_shapes=scratch,
        compiler_params=pltpu.CompilerParams(
            collective_id=0, has_side_effects=True, vmem_limit_bytes=60 * 1024 * 1024
        ),
    )(
        alpha_lists.T,
        beta_lists.T,
        coefficients.reshape(GROUPS, 16, COLS),
        diagonal,
        alpha_blocks,
        beta_blocks,
    )


def solution(mesh):
    in_specs = (
        P("alpha", "beta"),
        P("alpha", "beta"),
        P("alpha", None, None, None),
        P(),
        P("beta", None, None, None),
        P(),
    )
    return jax.shard_map(
        per_device, mesh=mesh, in_specs=in_specs, out_specs=P("alpha", "beta"), check_vma=False
    )
```

```python
import jax
import jax.numpy as jnp
from jax import lax
from jax.experimental import pallas as pl
from jax.experimental.pallas import tpu as pltpu
from jax.sharding import PartitionSpec as P

MESH = pl.DeviceIdType.MESH
BLK = 128
SLOTS = 14
RA = 4
RB = 8
CAP_A = 2
CAP_B = 4
ROWS = RA * BLK
COLS = RB * BLK
GROUPS = ROWS // 16
PER = BLK // 16

PIECES = {
    "n": (0, 18),
    "n0": (0, 9),
    "n1": (9, 9),
    "f": (18, 14),
    "f0": (18, 7),
    "f1": (25, 7),
}
PARTS = (PIECES["n"], PIECES["f"])
NSEM = 96

INV_A = 0
INV_B = 8
SEL_A = 40
SEL_B = 56
SEL_NEAR = {"xi": 88, "z1": 104, "z3": 120}
TABLE = 136


def body(la_hbm, lb_hbm, c_hbm, diag_hbm, ab_hbm, bb_hbm, out_ref, *scratch):
    it = iter(scratch)
    own, own_cb = next(it), next(it)
    gathered = {}
    for dx in range(2):
        for dz in range(4):
            for dc in range(2):
                if (dx, dz, dc) != (0, 0, 0) and dz != 2:
                    gathered[dx, dz, dc] = next(it)
    far = [[next(it) for _ in range(2)] for _ in range(2)]
    leaf_z, leaf_x, pick_z, pick_x = ([next(it) for _ in range(2)] for _ in range(4))
    peer = [next(it), next(it)]
    peer_cb = [next(it), next(it)]
    message = {(q, dy): next(it) for q in range(2) for dy in (1, 2, 3)}
    staged = {(q, dy): next(it) for q in range(2) for dy in (1, 2, 3)}
    la, lb, lists_a, lists_b, table, tab, ablk, bblk, diag, acc, wa, wb, xa, xb = (next(it) for _ in range(14))
    send_sems, recv_sems, local_sems = it

    ia, ib = lax.axis_index("alpha"), lax.axis_index("beta")
    x_lo, z, core = ia // 8, (ia // 2) % 4, ia % 2
    x_hi, y = ib // 4, ib % 4

    def alpha_at(dx, dz, dc):
        return ((x_lo + dx) % 2) * 8 + ((z + dz) % 4) * 2 + (core + dc) % 2

    def beta_at(dxh, dy):
        return ((x_hi + dxh) % 2) * 4 + (y + dy) % 4

    target = {
        "s": (alpha_at(0, 0, 1), ib),
        "xi": (alpha_at(1, 0, 0), ib),
        "xo": (alpha_at(1, 0, 0), beta_at(1, 0)),
        "z1": (alpha_at(0, 1, 0), ib),
        "z3": (alpha_at(0, 3, 0), ib),
        "y1": (ia, beta_at(0, 1)),
        "y3": (ia, beta_at(0, 3)),
        "y2": (ia, beta_at(0, 2)),
    }
    started = []

    def send(link, src, dst):
        n = len(started)
        copy = pltpu.make_async_remote_copy(
            src_ref=src,
            dst_ref=dst,
            send_sem=send_sems.at[n],
            recv_sem=recv_sems.at[n],
            device_id=target[link],
            device_id_type=MESH,
        )
        copy.start()
        started.append(copy)
        return copy

    def part(ref, piece):
        first, size = PIECES[piece]
        return ref.at[pl.ds(first, size)]

    def local(n, src, dst):
        copy = pltpu.make_async_copy(src, dst, local_sems.at[n])
        copy.start()
        return copy

    load_la = local(0, la_hbm, la)
    load_lb = local(1, lb_hbm, lb)
    load_own = local(2, c_hbm, own)
    barrier = pltpu.get_barrier_semaphore()
    for link in target:
        pl.semaphore_signal(barrier, inc=1, device_id=target[link], device_id_type=MESH)
    load_b = local(3, bb_hbm, bblk.at[:, pl.ds(0, SLOTS)])
    load_d = local(4, diag_hbm, diag)
    load_a = local(5, ab_hbm, ablk.at[:, pl.ds(0, SLOTS)])
    pl.semaphore_wait(barrier, len(target))

    xi, zn, zf, zs, sib = {}, {}, {}, {}, {}
    for p in ("n0", "n1", "f0", "f1"):
        xi[p] = send("xi", part(c_hbm, p), part(gathered[1, 0, 0], p))
    zo = {}
    for dz, order in ((1, ("f", "n")), (3, ("n", "f"))):
        for p in order:
            zo[dz, p] = send(f"z{dz}", part(c_hbm, p), part(gathered[0, dz, 0], p))
    sib[0, 0] = [send("s", c_hbm, gathered[0, 0, 1])]

    def to_sibling(dx, dz, p):
        copy = send("s", part(gathered[dx, dz, 0], p), part(gathered[dx, dz, 1], p))
        sib.setdefault((dx, dz), []).append(copy)

    lane = lax.broadcasted_iota(jnp.int32, (8, BLK), 1)

    def slots_of(lists):
        inv = jnp.full((8, BLK), SLOTS, jnp.int32)
        for k in range(SLOTS):
            inv = jnp.where(lists[:, k : k + 1] == lane, k, inv)
        return inv

    def picks_of(needed, per, cap, first_row):
        place = lane % per
        shifts = [1 << i for i in range(per.bit_length() - 1)]
        rank = needed
        for shift in shifts:
            rank = rank + jnp.where(place >= shift, pltpu.roll(rank, shift, 1), 0)
        rank = rank - needed
        for s in range(cap):
            pick = jnp.where((needed > 0) & (rank == s), lane, BLK - 1)
            for shift in shifts:
                moved = pltpu.roll(pick, BLK - shift, 1)
                pick = jnp.minimum(pick, jnp.where(place + shift < per, moved, BLK - 1))
            table[first_row + 8 * s : first_row + 8 * s + 8, :] = pick

    load_la.wait()
    load_lb.wait()
    lists_a[...] = la[...].T
    lists_b[...] = lb[...].T
    row = lax.broadcasted_iota(jnp.int32, (8, BLK), 0)
    for first_row, device in [(SEL_A, ia)] + [(SEL_NEAR[link], target[link][0]) for link in SEL_NEAR]:
        inv = slots_of(lists_a[pl.ds(pl.multiple_of((device // 2) * 8, 8), 8), :])
        if first_row == SEL_A:
            table[INV_A : INV_A + 8, :] = inv
        mine = (row // RA == core) & (inv < SLOTS)
        needed = jnp.broadcast_to(jnp.max(jnp.where(mine, 1, 0), axis=0, keepdims=True), (8, BLK))
        picks_of(needed, RA, CAP_A, first_row)
    needed = jnp.zeros((8, BLK), jnp.int32)
    for d in range(4):
        inv = slots_of(lists_b[pl.ds(pl.multiple_of(x_hi * 32 + d * 8, 8), 8), :])
        table[INV_B + 8 * d : INV_B + 8 * d + 8, :] = inv
        used = jnp.max(jnp.where(inv < SLOTS, 1, 0), axis=0, keepdims=True)
        needed = jnp.where(row == d, used, needed)
    picks_of(needed, RB, CAP_B, SEL_B)

    def by_column(src, dst, groups):
        def group(t, carry):
            for j in range(RB):
                dst[j, pl.ds(pl.multiple_of(t * 16, 16), 16), :] = src[t, :, j * BLK : (j + 1) * BLK]
            return carry

        lax.fori_loop(0, groups, group, 0)

    for r in range(RA):
        ablk[r, SLOTS] = jnp.zeros((BLK, BLK), jnp.bfloat16)
    for r in range(RB):
        bblk[r, SLOTS] = jnp.zeros((BLK, BLK), jnp.bfloat16)
    load_own.wait()
    load_tab = local(6, table, tab)
    by_column(own, own_cb, GROUPS)
    load_tab.wait()

    def pick_b(d, q, s):
        return tab[SEL_B + 8 * s + (y + d) % 4, beta_at(q, 0) * RB] % RB

    sent_b = {}

    def stage_own():
        for dy in (2, 1, 3):
            for s in range(CAP_B):
                staged[0, dy][s] = own_cb[pick_b(dy, 0, s)]

    def send_own():
        for dy in (2, 1, 3):
            sent_b[0, dy] = [send(f"y{dy}", staged[0, dy], message[0, dy])]

    def stage_peer(h):
        for dy in (2, 1, 3):
            for s in range(CAP_B):
                staged[1, dy][s, pl.ds(PARTS[h][0] * 16, PARTS[h][1] * 16), :] = peer_cb[h][pick_b(dy, 1, s)]

    def send_peer(h):
        for dy in (2, 1, 3):
            at = (slice(None), pl.ds(PARTS[h][0] * 16, PARTS[h][1] * 16))
            copy = send(f"y{dy}", staged[1, dy].at[at], message[1, dy].at[at])
            sent_b.setdefault((1, dy), []).append(copy)

    def alpha_weights(dx, dz):
        for dc in range(2):
            owner = alpha_at(dx, 4 - dz, dc)
            for s in range(CAP_A):
                column = (dc * CAP_A + s) * BLK
                pick = tab[SEL_A + 8 * s, owner * RA]
                for r in range(RA):
                    wa[r * BLK : (r + 1) * BLK, column : column + BLK] = ablk[r, tab[INV_A + core * RA + r, pick]]

    def alpha_inputs(dx, dz, *lanes):
        for dc in lanes:
            owner = alpha_at(dx, 4 - dz, dc)
            for s in range(CAP_A):
                block = tab[SEL_A + 8 * s, owner * RA] % RA
                for t in range(PER):
                    at = (dc * CAP_A + s) * BLK + t * 16
                    half, u = t // (PER // 2), t % (PER // 2)
                    if (dx, dz) == (1, 2):
                        rows = (leaf_z, leaf_x)[half][dc][s, u]
                    elif dz == 2:
                        rows = far[half][dc][block, u]
                    else:
                        source = own if (dx, dz, dc) == (0, 0, 0) else gathered[dx, dz, dc]
                        rows = source[block * PER + t]
                    xa[at : at + 16, :] = rows

    def alpha_dot(*lanes):
        depth = pl.ds(lanes[0] * CAP_A * BLK, len(lanes) * CAP_A * BLK)
        return jnp.dot(wa[:, depth], xa[depth, :], preferred_element_type=jnp.float32)

    def add_alpha(*lanes):
        acc[...] += alpha_dot(*lanes)

    def add_beta():
        acc[...] += lax.dot_general(
            xb[...], wb[...], (((1,), (1,)), ((), ())), preferred_element_type=jnp.float32
        )

    def alpha_chip(dx, dz):
        alpha_weights(dx, dz)
        alpha_inputs(dx, dz, 0, 1)
        add_alpha(0, 1)

    def beta_owner(q, dy):
        owner = beta_at(q, 4 - dy)
        for s in range(CAP_B):
            pick = tab[SEL_B + 8 * s + y, owner * RB]
            for r in range(RB):
                wb[r * BLK : (r + 1) * BLK, s * BLK : (s + 1) * BLK] = bblk[r, tab[INV_B + y * RB + r, pick]]
            column = slice(s * BLK, (s + 1) * BLK)
            if dy:
                xb[:, column] = message[q, dy][s]
            elif q:
                for h in range(2):
                    xb[pl.ds(PARTS[h][0] * 16, PARTS[h][1] * 16), column] = peer_cb[h][pick % RB]
            else:
                xb[:, column] = own_cb[pick % RB]
        add_beta()

    def arrived(copies):
        for copy in copies:
            copy.wait_recv()

    stage_own()
    send_own()
    load_d.wait()

    def init(n, carry):
        at = pl.ds(pl.multiple_of(n * 64, 64), 64)
        acc[at, :] = diag[at, :] * own[pl.ds(n * 4, 4)].astype(jnp.float32).reshape(64, COLS)
        return carry

    lax.fori_loop(0, ROWS // 64, init, 0)
    load_b.wait()
    load_a.wait()
    beta_owner(0, 0)
    arrived(sib[0, 0])
    alpha_chip(0, 0)

    xo = {}

    def over_x(p):
        h = int(p in ("f0", "f1"))
        first, size = PIECES[p]
        xi[p].wait_recv()
        xo[p] = send("xo", part(gathered[1, 0, 0], p), peer[h].at[pl.ds(first - PARTS[h][0], size)])

    zx, zfar, xleaf, zleaf = {}, {}, {}, {}

    def relay(half):
        for i in range(2):
            for dz, block in ((1, 2 + i), (3, i)):
                rows = gathered[0, dz, 0].at[pl.ds(block * PER + half * (PER // 2), PER // 2)]
                zfar[half, block] = send(f"z{dz}", rows, far[half][0].at[block])

    def far_to_sibling(half):
        for block in (2, 0, 3, 1):
            zfar[half, block].wait_recv()
            copy = send("s", far[half][0].at[block], far[half][1].at[block])
            sib.setdefault((0, 2, half), []).append(copy)

    def after(copies, dx, dz, *pieces):
        for p in pieces:
            copies[dz, p].wait_recv()
            to_sibling(dx, dz, p)

    def x_after_z(dz, p):
        zx[dz, p] = send("xi", part(gathered[0, dz, 0], p), part(gathered[1, dz, 0], p))

    def picked_for(link, s, dx, dz, dc):
        return tab[SEL_NEAR[link] + 8 * s, alpha_at(dx, 4 - dz, dc) * RA] % RA

    def stage_x():
        for dc in range(2):
            for s in range(CAP_A):
                block = picked_for("xi", s, 0, 2, dc)
                for t in range(PER // 2):
                    pick_x[dc][s, t] = far[1][dc][block, t]

    def send_x():
        for dc in range(2):
            xleaf[dc] = send("xi", pick_x[dc], leaf_x[dc])

    def stage_z():
        for dc, dz in enumerate((1, 3)):
            for s in range(CAP_A):
                first = picked_for(f"z{dz}", s, 1, dz, dc) * PER
                for t in range(PER // 2):
                    pick_z[dc][s, t] = gathered[1, dz, dc][first + t]

    def send_z():
        for dc, dz in enumerate((1, 3)):
            zleaf[dc] = send(f"z{dz}", pick_z[dc], leaf_z[dc])

    def over_x(p):
        h = int(p in ("f0", "f1"))
        first, size = PIECES[p]
        xi[p].wait_recv()
        xo[p] = send("xo", part(gathered[1, 0, 0], p), peer[h].at[pl.ds(first - PARTS[h][0], size)])

    over_x("n0")
    after(zo, 0, 1, "f")
    x_after_z(1, "f0")
    after(zo, 0, 3, "n")
    relay(1)
    over_x("n1")
    for dz in (1, 3):
        zx[dz, "n"] = send(f"z{dz}", part(gathered[1, 0, 0], "n"), part(gathered[1, dz, 0], "n"))
    to_sibling(1, 0, "n")
    arrived(sent_b[0, 2])
    beta_owner(0, 2)
    over_x("f0")
    arrived([xo["n0"], xo["n1"]])
    by_column(peer[0], peer_cb[0], PARTS[0][1])
    stage_peer(0)
    send_peer(0)
    after(zo, 0, 3, "f")
    x_after_z(3, "f")
    x_after_z(1, "f1")
    after(zo, 0, 1, "n")
    relay(0)
    over_x("f1")
    to_sibling(1, 0, "f")
    arrived(sent_b[0, 1])
    beta_owner(0, 1)
    arrived(sent_b[0, 3])
    beta_owner(0, 3)
    far_to_sibling(1)
    after(zx, 1, 1, "f0")
    arrived([xo["f0"], xo["f1"]])
    by_column(peer[1], peer_cb[1], PARTS[1][1])
    stage_peer(1)
    arrived(sib[0, 2, 1])
    send_peer(1)
    stage_x()
    arrived(sib[1, 0])
    alpha_chip(1, 0)
    send_x()
    arrived(sib[0, 1])
    alpha_chip(0, 1)
    beta_owner(1, 0)
    arrived(sib[0, 3])
    alpha_chip(0, 3)
    after(zx, 1, 3, "f", "n")
    after(zx, 1, 1, "n", "f1")
    arrived(sib[1, 3])
    stage_z()
    arrived(sib[1, 1])
    alpha_weights(1, 1)
    alpha_inputs(1, 1, 0, 1)
    send_z()
    add_alpha(0, 1)
    alpha_chip(1, 3)
    far_to_sibling(0)
    arrived(sib[0, 2, 0])
    alpha_chip(0, 2)
    arrived(sent_b[1, 2])
    beta_owner(1, 2)
    arrived(sent_b[1, 1])
    beta_owner(1, 1)
    arrived(sent_b[1, 3])
    beta_owner(1, 3)
    alpha_weights(1, 2)
    arrived([zleaf[0], zleaf[1], xleaf[0]])
    alpha_inputs(1, 2, 0)
    add_alpha(0)
    arrived([xleaf[1]])
    alpha_inputs(1, 2, 1)

    out_ref[...] = (acc[...] + alpha_dot(1)).astype(jnp.bfloat16)
    for copy in started:
        copy.wait_send()
    assert len(started) <= NSEM, len(started)


def per_device(coefficients, diagonal, alpha_blocks, alpha_lists, beta_blocks, beta_lists):
    grouped = pltpu.VMEM((GROUPS, 16, COLS), jnp.bfloat16)
    halves = pltpu.VMEM((RA, PER // 2, 16, COLS), jnp.bfloat16)
    picked = pltpu.VMEM((CAP_A, PER // 2, 16, COLS), jnp.bfloat16)
    by_block = pltpu.VMEM((RB, ROWS, BLK), jnp.bfloat16)
    slots = pltpu.VMEM((CAP_B, ROWS, BLK), jnp.bfloat16)
    scratch = [grouped, by_block] + [grouped] * 11 + [halves] * 4 + [picked] * 8 + [pltpu.VMEM((n, 16, COLS), jnp.bfloat16) for _, n in PARTS]
    scratch += [pltpu.VMEM((RB, n * 16, BLK), jnp.bfloat16) for _, n in PARTS] + [slots] * 12
    scratch += [
        pltpu.VMEM((SLOTS, 64), jnp.int32),
        pltpu.VMEM((SLOTS, 64), jnp.int32),
        pltpu.VMEM((64, SLOTS), jnp.int32),
        pltpu.VMEM((64, SLOTS), jnp.int32),
        pltpu.VMEM((TABLE, BLK), jnp.int32),
        pltpu.SMEM((TABLE, BLK), jnp.int32),
        pltpu.VMEM((RA, SLOTS + 1, BLK, BLK), jnp.bfloat16),
        pltpu.VMEM((RB, SLOTS + 1, BLK, BLK), jnp.bfloat16),
        pltpu.VMEM((ROWS, COLS), jnp.float32),
        pltpu.VMEM((ROWS, COLS), jnp.float32),
        pltpu.VMEM((ROWS, 4 * BLK), jnp.bfloat16),
        pltpu.VMEM((COLS, 4 * BLK), jnp.bfloat16),
        pltpu.VMEM((4 * BLK, COLS), jnp.bfloat16),
        pltpu.VMEM((ROWS, 4 * BLK), jnp.bfloat16),
        pltpu.SemaphoreType.DMA((NSEM,)),
        pltpu.SemaphoreType.DMA((NSEM,)),
        pltpu.SemaphoreType.DMA((7,)),
    ]
    return pl.pallas_call(
        body,
        out_shape=pltpu.VMEM((ROWS, COLS), jnp.bfloat16),
        in_specs=[pl.BlockSpec(memory_space=pl.ANY)] * 6,
        out_specs=pl.BlockSpec(memory_space=pltpu.VMEM),
        scratch_shapes=scratch,
        compiler_params=pltpu.CompilerParams(
            collective_id=0, has_side_effects=True, vmem_limit_bytes=60 * 1024 * 1024
        ),
    )(
        alpha_lists.T,
        beta_lists.T,
        coefficients.reshape(GROUPS, 16, COLS),
        diagonal,
        alpha_blocks,
        beta_blocks,
    )


def solution(mesh):
    in_specs = (
        P("alpha", "beta"),
        P("alpha", "beta"),
        P("alpha", None, None, None),
        P(),
        P("beta", None, None, None),
        P(),
    )
    return jax.shard_map(
        per_device, mesh=mesh, in_specs=in_specs, out_specs=P("alpha", "beta"), check_vma=False
    )
```

```python
import jax
import jax.numpy as jnp
from jax import lax
from jax.experimental import pallas as pl
from jax.experimental.pallas import tpu as pltpu
from jax.sharding import PartitionSpec as P

MESH = pl.DeviceIdType.MESH
BLK = 128
SLOTS = 14
RA = 4
RB = 8
CAP_A = 2
CAP_B = 4
ROWS = RA * BLK
COLS = RB * BLK
GROUPS = ROWS // 16
PER = BLK // 16

PIECES = {
    "n": (0, 18),
    "n0": (0, 9),
    "n1": (9, 9),
    "f": (18, 14),
    "f0": (18, 7),
    "f1": (25, 7),
}
PARTS = (PIECES["n"], PIECES["f"])
NSEM = 96

INV_A = 0
INV_B = 8
SEL_A = 40
SEL_B = 56
SEL_NEAR = {"xi": 88, "z1": 104, "z3": 120}
TABLE = 136


def body(la_hbm, lb_hbm, c_hbm, diag_hbm, ab_hbm, bb_hbm, out_ref, *scratch):
    it = iter(scratch)
    own, own_cb = next(it), next(it)
    gathered = {}
    for dx in range(2):
        for dz in range(4):
            for dc in range(2):
                if (dx, dz, dc) != (0, 0, 0) and dz != 2:
                    gathered[dx, dz, dc] = next(it)
    far = [[next(it) for _ in range(2)] for _ in range(2)]
    leaf_z, leaf_x, pick_z, pick_x = ([next(it) for _ in range(2)] for _ in range(4))
    peer = [next(it), next(it)]
    peer_cb = [next(it), next(it)]
    message = {(q, dy): next(it) for q in range(2) for dy in (1, 2, 3)}
    staged = {(q, dy): next(it) for q in range(2) for dy in (1, 2, 3)}
    la, lb, lists_a, lists_b, table, tab, ablk, bblk, diag, acc, wa, wb, xa, xb = (next(it) for _ in range(14))
    send_sems, recv_sems, local_sems = it

    ia, ib = lax.axis_index("alpha"), lax.axis_index("beta")
    x_lo, z, core = ia // 8, (ia // 2) % 4, ia % 2
    x_hi, y = ib // 4, ib % 4

    def alpha_at(dx, dz, dc):
        return ((x_lo + dx) % 2) * 8 + ((z + dz) % 4) * 2 + (core + dc) % 2

    def beta_at(dxh, dy):
        return ((x_hi + dxh) % 2) * 4 + (y + dy) % 4

    target = {
        "s": (alpha_at(0, 0, 1), ib),
        "xi": (alpha_at(1, 0, 0), ib),
        "xo": (alpha_at(1, 0, 0), beta_at(1, 0)),
        "z1": (alpha_at(0, 1, 0), ib),
        "z3": (alpha_at(0, 3, 0), ib),
        "y1": (ia, beta_at(0, 1)),
        "y3": (ia, beta_at(0, 3)),
        "y2": (ia, beta_at(0, 2)),
    }
    started = []

    def send(link, src, dst):
        n = len(started)
        copy = pltpu.make_async_remote_copy(
            src_ref=src,
            dst_ref=dst,
            send_sem=send_sems.at[n],
            recv_sem=recv_sems.at[n],
            device_id=target[link],
            device_id_type=MESH,
        )
        copy.start()
        started.append(copy)
        return copy

    def part(ref, piece):
        first, size = PIECES[piece]
        return ref.at[pl.ds(first, size)]

    def local(n, src, dst):
        copy = pltpu.make_async_copy(src, dst, local_sems.at[n])
        copy.start()
        return copy

    load_la = local(0, la_hbm, la)
    load_lb = local(1, lb_hbm, lb)
    load_own = local(2, c_hbm, own)
    barrier = pltpu.get_barrier_semaphore()
    for link in target:
        pl.semaphore_signal(barrier, inc=1, device_id=target[link], device_id_type=MESH)
    load_b = local(3, bb_hbm, bblk.at[:, pl.ds(0, SLOTS)])
    load_d = local(4, diag_hbm, diag)
    load_a = local(5, ab_hbm, ablk.at[:, pl.ds(0, SLOTS)])
    pl.semaphore_wait(barrier, len(target))

    xi, zn, zf, zs, sib = {}, {}, {}, {}, {}
    for p in ("n0", "n1", "f0", "f1"):
        xi[p] = send("xi", part(c_hbm, p), part(gathered[1, 0, 0], p))
    zo = {}
    for dz, order in ((1, ("f", "n")), (3, ("n", "f"))):
        for p in order:
            zo[dz, p] = send(f"z{dz}", part(c_hbm, p), part(gathered[0, dz, 0], p))
    sib[0, 0] = [send("s", c_hbm, gathered[0, 0, 1])]

    def to_sibling(dx, dz, p):
        copy = send("s", part(gathered[dx, dz, 0], p), part(gathered[dx, dz, 1], p))
        sib.setdefault((dx, dz), []).append(copy)

    lane = lax.broadcasted_iota(jnp.int32, (8, BLK), 1)

    def slots_of(lists):
        inv = jnp.full((8, BLK), SLOTS, jnp.int32)
        for k in range(SLOTS):
            inv = jnp.where(lists[:, k : k + 1] == lane, k, inv)
        return inv

    def picks_of(needed, per, cap, first_row):
        place = lane % per
        shifts = [1 << i for i in range(per.bit_length() - 1)]
        rank = needed
        for shift in shifts:
            rank = rank + jnp.where(place >= shift, pltpu.roll(rank, shift, 1), 0)
        rank = rank - needed
        for s in range(cap):
            pick = jnp.where((needed > 0) & (rank == s), lane, BLK - 1)
            for shift in shifts:
                moved = pltpu.roll(pick, BLK - shift, 1)
                pick = jnp.minimum(pick, jnp.where(place + shift < per, moved, BLK - 1))
            table[first_row + 8 * s : first_row + 8 * s + 8, :] = pick

    load_la.wait()
    load_lb.wait()
    lists_a[...] = la[...].T
    lists_b[...] = lb[...].T
    row = lax.broadcasted_iota(jnp.int32, (8, BLK), 0)
    for first_row, device in [(SEL_A, ia)] + [(SEL_NEAR[link], target[link][0]) for link in SEL_NEAR]:
        inv = slots_of(lists_a[pl.ds(pl.multiple_of((device // 2) * 8, 8), 8), :])
        if first_row == SEL_A:
            table[INV_A : INV_A + 8, :] = inv
        mine = (row // RA == core) & (inv < SLOTS)
        needed = jnp.broadcast_to(jnp.max(jnp.where(mine, 1, 0), axis=0, keepdims=True), (8, BLK))
        picks_of(needed, RA, CAP_A, first_row)
    needed = jnp.zeros((8, BLK), jnp.int32)
    for d in range(4):
        inv = slots_of(lists_b[pl.ds(pl.multiple_of(x_hi * 32 + d * 8, 8), 8), :])
        table[INV_B + 8 * d : INV_B + 8 * d + 8, :] = inv
        used = jnp.max(jnp.where(inv < SLOTS, 1, 0), axis=0, keepdims=True)
        needed = jnp.where(row == d, used, needed)
    picks_of(needed, RB, CAP_B, SEL_B)

    def by_column(src, dst, groups):
        def group(t, carry):
            for j in range(RB):
                dst[j, pl.ds(pl.multiple_of(t * 16, 16), 16), :] = src[t, :, j * BLK : (j + 1) * BLK]
            return carry

        lax.fori_loop(0, groups, group, 0)

    for r in range(RA):
        ablk[r, SLOTS] = jnp.zeros((BLK, BLK), jnp.bfloat16)
    for r in range(RB):
        bblk[r, SLOTS] = jnp.zeros((BLK, BLK), jnp.bfloat16)
    load_own.wait()
    load_tab = local(6, table, tab)
    by_column(own, own_cb, GROUPS)
    load_tab.wait()

    def pick_b(d, q, s):
        return tab[SEL_B + 8 * s + (y + d) % 4, beta_at(q, 0) * RB] % RB

    sent_b = {}

    def stage_own():
        for dy in (2, 1, 3):
            for s in range(CAP_B):
                staged[0, dy][s] = own_cb[pick_b(dy, 0, s)]

    def send_own():
        for dy in (2, 1, 3):
            sent_b[0, dy] = [send(f"y{dy}", staged[0, dy], message[0, dy])]

    def stage_peer(h):
        for dy in (2, 1, 3):
            for s in range(CAP_B):
                staged[1, dy][s, pl.ds(PARTS[h][0] * 16, PARTS[h][1] * 16), :] = peer_cb[h][pick_b(dy, 1, s)]

    def send_peer(h):
        for dy in (2, 1, 3):
            at = (slice(None), pl.ds(PARTS[h][0] * 16, PARTS[h][1] * 16))
            copy = send(f"y{dy}", staged[1, dy].at[at], message[1, dy].at[at])
            sent_b.setdefault((1, dy), []).append(copy)

    def alpha_weights(dx, dz):
        for dc in range(2):
            owner = alpha_at(dx, 4 - dz, dc)
            for s in range(CAP_A):
                column = (dc * CAP_A + s) * BLK
                pick = tab[SEL_A + 8 * s, owner * RA]
                for r in range(RA):
                    wa[r * BLK : (r + 1) * BLK, column : column + BLK] = ablk[r, tab[INV_A + core * RA + r, pick]]

    def alpha_inputs(dx, dz, *lanes):
        for dc in lanes:
            owner = alpha_at(dx, 4 - dz, dc)
            for s in range(CAP_A):
                block = tab[SEL_A + 8 * s, owner * RA] % RA
                for t in range(PER):
                    at = (dc * CAP_A + s) * BLK + t * 16
                    half, u = t // (PER // 2), t % (PER // 2)
                    if (dx, dz) == (1, 2):
                        rows = (leaf_z, leaf_x)[half][dc][s, u]
                    elif dz == 2:
                        rows = far[half][dc][block, u]
                    else:
                        source = own if (dx, dz, dc) == (0, 0, 0) else gathered[dx, dz, dc]
                        rows = source[block * PER + t]
                    xa[at : at + 16, :] = rows

    def alpha_dot(*lanes):
        depth = pl.ds(lanes[0] * CAP_A * BLK, len(lanes) * CAP_A * BLK)
        return jnp.dot(wa[:, depth], xa[depth, :], preferred_element_type=jnp.float32)

    def add_alpha(*lanes):
        acc[...] += alpha_dot(*lanes)

    def add_beta():
        acc[...] += lax.dot_general(
            xb[...], wb[...], (((1,), (1,)), ((), ())), preferred_element_type=jnp.float32
        )

    def alpha_chip(dx, dz):
        alpha_weights(dx, dz)
        alpha_inputs(dx, dz, 0, 1)
        add_alpha(0, 1)

    def beta_owner(q, dy):
        owner = beta_at(q, 4 - dy)
        for s in range(CAP_B):
            pick = tab[SEL_B + 8 * s + y, owner * RB]
            for r in range(RB):
                wb[r * BLK : (r + 1) * BLK, s * BLK : (s + 1) * BLK] = bblk[r, tab[INV_B + y * RB + r, pick]]
            column = slice(s * BLK, (s + 1) * BLK)
            if dy:
                xb[:, column] = message[q, dy][s]
            elif q:
                for h in range(2):
                    xb[pl.ds(PARTS[h][0] * 16, PARTS[h][1] * 16), column] = peer_cb[h][pick % RB]
            else:
                xb[:, column] = own_cb[pick % RB]
        add_beta()

    def arrived(copies):
        for copy in copies:
            copy.wait_recv()

    stage_own()
    send_own()
    load_d.wait()

    def init(n, carry):
        at = pl.ds(pl.multiple_of(n * 64, 64), 64)
        acc[at, :] = diag[at, :] * own[pl.ds(n * 4, 4)].astype(jnp.float32).reshape(64, COLS)
        return carry

    lax.fori_loop(0, ROWS // 64, init, 0)
    load_b.wait()
    load_a.wait()
    beta_owner(0, 0)
    arrived(sib[0, 0])
    alpha_chip(0, 0)

    xo = {}

    def over_x(p):
        h = int(p in ("f0", "f1"))
        first, size = PIECES[p]
        xi[p].wait_recv()
        xo[p] = send("xo", part(gathered[1, 0, 0], p), peer[h].at[pl.ds(first - PARTS[h][0], size)])

    zx, zfar, xleaf, zleaf = {}, {}, {}, {}

    def relay(half):
        for i in range(2):
            for dz, block in ((1, 2 + i), (3, i)):
                rows = gathered[0, dz, 0].at[pl.ds(block * PER + half * (PER // 2), PER // 2)]
                zfar[half, block] = send(f"z{dz}", rows, far[half][0].at[block])

    def far_to_sibling(half):
        for block in (2, 0, 3, 1):
            zfar[half, block].wait_recv()
            copy = send("s", far[half][0].at[block], far[half][1].at[block])
            sib.setdefault((0, 2, half), []).append(copy)

    def after(copies, dx, dz, *pieces):
        for p in pieces:
            copies[dz, p].wait_recv()
            to_sibling(dx, dz, p)

    def x_after_z(dz, p):
        zx[dz, p] = send("xi", part(gathered[0, dz, 0], p), part(gathered[1, dz, 0], p))

    def picked_for(link, s, dx, dz, dc):
        return tab[SEL_NEAR[link] + 8 * s, alpha_at(dx, 4 - dz, dc) * RA] % RA

    def stage_x():
        for dc in range(2):
            for s in range(CAP_A):
                block = picked_for("xi", s, 0, 2, dc)
                for t in range(PER // 2):
                    pick_x[dc][s, t] = far[1][dc][block, t]

    def send_x():
        for dc in range(2):
            xleaf[dc] = send("xi", pick_x[dc], leaf_x[dc])

    def stage_z(dc):
        dz = (1, 3)[dc]
        for s in range(CAP_A):
            first = picked_for(f"z{dz}", s, 1, dz, dc) * PER
            for t in range(PER // 2):
                pick_z[dc][s, t] = gathered[1, dz, dc][first + t]

    def send_z(dc):
        zleaf[dc] = send(f"z{(1, 3)[dc]}", pick_z[dc], leaf_z[dc])

    def over_x(p):
        h = int(p in ("f0", "f1"))
        first, size = PIECES[p]
        xi[p].wait_recv()
        xo[p] = send("xo", part(gathered[1, 0, 0], p), peer[h].at[pl.ds(first - PARTS[h][0], size)])

    over_x("n0")
    after(zo, 0, 1, "f")
    x_after_z(1, "f0")
    after(zo, 0, 3, "n")
    relay(1)
    over_x("n1")
    for dz in (1, 3):
        zx[dz, "n"] = send(f"z{dz}", part(gathered[1, 0, 0], "n"), part(gathered[1, dz, 0], "n"))
    to_sibling(1, 0, "n")
    arrived(sent_b[0, 2])
    beta_owner(0, 2)
    over_x("f0")
    arrived([xo["n0"], xo["n1"]])
    by_column(peer[0], peer_cb[0], PARTS[0][1])
    stage_peer(0)
    send_peer(0)
    after(zo, 0, 3, "f")
    x_after_z(3, "f")
    x_after_z(1, "f1")
    after(zo, 0, 1, "n")
    relay(0)
    over_x("f1")
    to_sibling(1, 0, "f")
    arrived(sent_b[0, 1])
    beta_owner(0, 1)
    arrived(sent_b[0, 3])
    beta_owner(0, 3)
    far_to_sibling(1)
    after(zx, 1, 1, "f0")
    arrived([xo["f0"], xo["f1"]])
    by_column(peer[1], peer_cb[1], PARTS[1][1])
    stage_peer(1)
    arrived(sib[0, 2, 1])
    send_peer(1)
    stage_x()
    arrived(sib[1, 0])
    alpha_chip(1, 0)
    send_x()
    arrived(sib[0, 1])
    alpha_chip(0, 1)
    beta_owner(1, 0)
    arrived(sib[0, 3])
    alpha_chip(0, 3)
    after(zx, 1, 3, "f", "n")
    after(zx, 1, 1, "n")
    arrived(sib[1, 3])
    stage_z(1)
    alpha_weights(1, 3)
    send_z(1)
    alpha_inputs(1, 3, 0, 1)
    add_alpha(0, 1)
    after(zx, 1, 1, "f1")
    stage_z(0)
    alpha_weights(1, 1)
    send_z(0)
    arrived(sib[1, 1])
    alpha_inputs(1, 1, 0, 1)
    add_alpha(0, 1)
    far_to_sibling(0)
    arrived(sib[0, 2, 0])
    alpha_chip(0, 2)
    arrived(sent_b[1, 2])
    beta_owner(1, 2)
    arrived(sent_b[1, 1])
    beta_owner(1, 1)
    arrived(sent_b[1, 3])
    beta_owner(1, 3)
    alpha_weights(1, 2)
    arrived([zleaf[0], xleaf[0]])
    alpha_inputs(1, 2, 0)
    add_alpha(0)
    arrived([zleaf[1], xleaf[1]])
    alpha_inputs(1, 2, 1)

    out_ref[...] = (acc[...] + alpha_dot(1)).astype(jnp.bfloat16)
    for copy in started:
        copy.wait_send()
    assert len(started) <= NSEM, len(started)


def per_device(coefficients, diagonal, alpha_blocks, alpha_lists, beta_blocks, beta_lists):
    grouped = pltpu.VMEM((GROUPS, 16, COLS), jnp.bfloat16)
    halves = pltpu.VMEM((RA, PER // 2, 16, COLS), jnp.bfloat16)
    picked = pltpu.VMEM((CAP_A, PER // 2, 16, COLS), jnp.bfloat16)
    by_block = pltpu.VMEM((RB, ROWS, BLK), jnp.bfloat16)
    slots = pltpu.VMEM((CAP_B, ROWS, BLK), jnp.bfloat16)
    scratch = [grouped, by_block] + [grouped] * 11 + [halves] * 4 + [picked] * 8 + [pltpu.VMEM((n, 16, COLS), jnp.bfloat16) for _, n in PARTS]
    scratch += [pltpu.VMEM((RB, n * 16, BLK), jnp.bfloat16) for _, n in PARTS] + [slots] * 12
    scratch += [
        pltpu.VMEM((SLOTS, 64), jnp.int32),
        pltpu.VMEM((SLOTS, 64), jnp.int32),
        pltpu.VMEM((64, SLOTS), jnp.int32),
        pltpu.VMEM((64, SLOTS), jnp.int32),
        pltpu.VMEM((TABLE, BLK), jnp.int32),
        pltpu.SMEM((TABLE, BLK), jnp.int32),
        pltpu.VMEM((RA, SLOTS + 1, BLK, BLK), jnp.bfloat16),
        pltpu.VMEM((RB, SLOTS + 1, BLK, BLK), jnp.bfloat16),
        pltpu.VMEM((ROWS, COLS), jnp.float32),
        pltpu.VMEM((ROWS, COLS), jnp.float32),
        pltpu.VMEM((ROWS, 4 * BLK), jnp.bfloat16),
        pltpu.VMEM((COLS, 4 * BLK), jnp.bfloat16),
        pltpu.VMEM((4 * BLK, COLS), jnp.bfloat16),
        pltpu.VMEM((ROWS, 4 * BLK), jnp.bfloat16),
        pltpu.SemaphoreType.DMA((NSEM,)),
        pltpu.SemaphoreType.DMA((NSEM,)),
        pltpu.SemaphoreType.DMA((7,)),
    ]
    return pl.pallas_call(
        body,
        out_shape=pltpu.VMEM((ROWS, COLS), jnp.bfloat16),
        in_specs=[pl.BlockSpec(memory_space=pl.ANY)] * 6,
        out_specs=pl.BlockSpec(memory_space=pltpu.VMEM),
        scratch_shapes=scratch,
        compiler_params=pltpu.CompilerParams(
            collective_id=0, has_side_effects=True, vmem_limit_bytes=60 * 1024 * 1024
        ),
    )(
        alpha_lists.T,
        beta_lists.T,
        coefficients.reshape(GROUPS, 16, COLS),
        diagonal,
        alpha_blocks,
        beta_blocks,
    )


def solution(mesh):
    in_specs = (
        P("alpha", "beta"),
        P("alpha", "beta"),
        P("alpha", None, None, None),
        P(),
        P("beta", None, None, None),
        P(),
    )
    return jax.shard_map(
        per_device, mesh=mesh, in_specs=in_specs, out_specs=P("alpha", "beta"), check_vma=False
    )
```

```python
import jax
import jax.numpy as jnp
from jax import lax
from jax.experimental import pallas as pl
from jax.experimental.pallas import tpu as pltpu
from jax.sharding import PartitionSpec as P

MESH = pl.DeviceIdType.MESH
BLK = 128
SLOTS = 14
RA = 4
RB = 8
CAP_A = 2
CAP_B = 4
ROWS = RA * BLK
COLS = RB * BLK
GROUPS = ROWS // 16
PER = BLK // 16

PIECES = {
    "n": (0, 18),
    "n0": (0, 9),
    "n1": (9, 9),
    "f": (18, 14),
    "f0": (18, 7),
    "f1": (25, 7),
}
PARTS = (PIECES["n"], PIECES["f"])
NSEM = 96

INV_A = 0
INV_B = 8
SEL_A = 40
SEL_B = 56
SEL_NEAR = {"xi": 88, "z1": 104, "z3": 120}
TABLE = 136


def body(la_hbm, lb_hbm, c_hbm, diag_hbm, ab_hbm, bb_hbm, out_ref, *scratch):
    it = iter(scratch)
    own, own_cb = next(it), next(it)
    gathered = {}
    for dx in range(2):
        for dz in range(4):
            for dc in range(2):
                if (dx, dz, dc) != (0, 0, 0) and dz != 2:
                    gathered[dx, dz, dc] = next(it)
    far = [[next(it) for _ in range(2)] for _ in range(2)]
    leaf_z, leaf_x, pick_z, pick_x = ([next(it) for _ in range(2)] for _ in range(4))
    peer = [next(it), next(it)]
    peer_cb = [next(it), next(it)]
    message = {(q, dy): next(it) for q in range(2) for dy in (1, 2, 3)}
    staged = {(q, dy): next(it) for q in range(2) for dy in (1, 2, 3)}
    la, lb, lists_a, lists_b, table, tab, ablk, bblk, diag, acc, wa, wb, xa, xb = (next(it) for _ in range(14))
    send_sems, recv_sems, local_sems = it

    ia, ib = lax.axis_index("alpha"), lax.axis_index("beta")
    x_lo, z, core = ia // 8, (ia // 2) % 4, ia % 2
    x_hi, y = ib // 4, ib % 4

    def alpha_at(dx, dz, dc):
        return ((x_lo + dx) % 2) * 8 + ((z + dz) % 4) * 2 + (core + dc) % 2

    def beta_at(dxh, dy):
        return ((x_hi + dxh) % 2) * 4 + (y + dy) % 4

    target = {
        "s": (alpha_at(0, 0, 1), ib),
        "xi": (alpha_at(1, 0, 0), ib),
        "xo": (alpha_at(1, 0, 0), beta_at(1, 0)),
        "z1": (alpha_at(0, 1, 0), ib),
        "z3": (alpha_at(0, 3, 0), ib),
        "y1": (ia, beta_at(0, 1)),
        "y3": (ia, beta_at(0, 3)),
        "y2": (ia, beta_at(0, 2)),
    }
    started = []

    def send(link, src, dst):
        n = len(started)
        copy = pltpu.make_async_remote_copy(
            src_ref=src,
            dst_ref=dst,
            send_sem=send_sems.at[n],
            recv_sem=recv_sems.at[n],
            device_id=target[link],
            device_id_type=MESH,
        )
        copy.start()
        started.append(copy)
        return copy

    def part(ref, piece):
        first, size = PIECES[piece]
        return ref.at[pl.ds(first, size)]

    def local(n, src, dst):
        copy = pltpu.make_async_copy(src, dst, local_sems.at[n])
        copy.start()
        return copy

    load_la = local(0, la_hbm, la)
    load_lb = local(1, lb_hbm, lb)
    load_own = local(2, c_hbm, own)
    barrier = pltpu.get_barrier_semaphore()
    for link in target:
        pl.semaphore_signal(barrier, inc=1, device_id=target[link], device_id_type=MESH)
    load_b = local(3, bb_hbm, bblk.at[:, pl.ds(0, SLOTS)])
    load_d = local(4, diag_hbm, diag)
    load_a = local(5, ab_hbm, ablk.at[:, pl.ds(0, SLOTS)])
    pl.semaphore_wait(barrier, len(target))

    xi, zn, zf, zs, sib = {}, {}, {}, {}, {}
    for p in ("n0", "n1", "f0", "f1"):
        xi[p] = send("xi", part(c_hbm, p), part(gathered[1, 0, 0], p))
    zo = {}
    for dz, order in ((1, ("f", "n")), (3, ("n", "f"))):
        for p in order:
            zo[dz, p] = send(f"z{dz}", part(c_hbm, p), part(gathered[0, dz, 0], p))
    sib[0, 0] = [send("s", c_hbm, gathered[0, 0, 1])]

    def to_sibling(dx, dz, p):
        copy = send("s", part(gathered[dx, dz, 0], p), part(gathered[dx, dz, 1], p))
        sib.setdefault((dx, dz), []).append(copy)

    lane = lax.broadcasted_iota(jnp.int32, (8, BLK), 1)

    def slots_of(lists):
        inv = jnp.full((8, BLK), SLOTS, jnp.int32)
        for k in range(SLOTS):
            inv = jnp.where(lists[:, k : k + 1] == lane, k, inv)
        return inv

    def picks_of(needed, per, cap, first_row):
        place = lane % per
        shifts = [1 << i for i in range(per.bit_length() - 1)]
        rank = needed
        for shift in shifts:
            rank = rank + jnp.where(place >= shift, pltpu.roll(rank, shift, 1), 0)
        rank = rank - needed
        for s in range(cap):
            pick = jnp.where((needed > 0) & (rank == s), lane, BLK - 1)
            for shift in shifts:
                moved = pltpu.roll(pick, BLK - shift, 1)
                pick = jnp.minimum(pick, jnp.where(place + shift < per, moved, BLK - 1))
            table[first_row + 8 * s : first_row + 8 * s + 8, :] = pick

    load_la.wait()
    load_lb.wait()
    lists_a[...] = la[...].T
    lists_b[...] = lb[...].T
    row = lax.broadcasted_iota(jnp.int32, (8, BLK), 0)
    for first_row, device in [(SEL_A, ia)] + [(SEL_NEAR[link], target[link][0]) for link in SEL_NEAR]:
        inv = slots_of(lists_a[pl.ds(pl.multiple_of((device // 2) * 8, 8), 8), :])
        if first_row == SEL_A:
            table[INV_A : INV_A + 8, :] = inv
        mine = (row // RA == core) & (inv < SLOTS)
        needed = jnp.broadcast_to(jnp.max(jnp.where(mine, 1, 0), axis=0, keepdims=True), (8, BLK))
        picks_of(needed, RA, CAP_A, first_row)
    needed = jnp.zeros((8, BLK), jnp.int32)
    for d in range(4):
        inv = slots_of(lists_b[pl.ds(pl.multiple_of(x_hi * 32 + d * 8, 8), 8), :])
        table[INV_B + 8 * d : INV_B + 8 * d + 8, :] = inv
        used = jnp.max(jnp.where(inv < SLOTS, 1, 0), axis=0, keepdims=True)
        needed = jnp.where(row == d, used, needed)
    picks_of(needed, RB, CAP_B, SEL_B)

    def by_column(src, dst, groups):
        def group(t, carry):
            for j in range(RB):
                dst[j, pl.ds(pl.multiple_of(t * 16, 16), 16), :] = src[t, :, j * BLK : (j + 1) * BLK]
            return carry

        lax.fori_loop(0, groups, group, 0)

    for r in range(RA):
        ablk[r, SLOTS] = jnp.zeros((BLK, BLK), jnp.bfloat16)
    load_own.wait()
    by_column(own, own_cb, GROUPS)
    load_tab = local(6, table, tab)
    load_tab.wait()

    def pick_b(d, q, s):
        return tab[SEL_B + 8 * s + (y + d) % 4, beta_at(q, 0) * RB] % RB

    sent_b = {}

    def stage_own():
        for dy in (2, 1, 3):
            for s in range(CAP_B):
                staged[0, dy][s] = own_cb[pick_b(dy, 0, s)]

    def send_own():
        for dy in (2, 1, 3):
            sent_b[0, dy] = [send(f"y{dy}", staged[0, dy], message[0, dy])]

    def stage_peer(h):
        for dy in (2, 1, 3):
            for s in range(CAP_B):
                staged[1, dy][s, pl.ds(PARTS[h][0] * 16, PARTS[h][1] * 16), :] = peer_cb[h][pick_b(dy, 1, s)]

    def send_peer(h):
        for dy in (2, 1, 3):
            at = (slice(None), pl.ds(PARTS[h][0] * 16, PARTS[h][1] * 16))
            copy = send(f"y{dy}", staged[1, dy].at[at], message[1, dy].at[at])
            sent_b.setdefault((1, dy), []).append(copy)

    def alpha_weights(dx, dz):
        for dc in range(2):
            owner = alpha_at(dx, 4 - dz, dc)
            for s in range(CAP_A):
                column = (dc * CAP_A + s) * BLK
                pick = tab[SEL_A + 8 * s, owner * RA]
                for r in range(RA):
                    wa[r * BLK : (r + 1) * BLK, column : column + BLK] = ablk[r, tab[INV_A + core * RA + r, pick]]

    def alpha_inputs(dx, dz, *lanes):
        for dc in lanes:
            owner = alpha_at(dx, 4 - dz, dc)
            for s in range(CAP_A):
                block = tab[SEL_A + 8 * s, owner * RA] % RA
                for t in range(PER):
                    at = (dc * CAP_A + s) * BLK + t * 16
                    half, u = t // (PER // 2), t % (PER // 2)
                    if (dx, dz) == (1, 2):
                        rows = (leaf_z, leaf_x)[half][dc][s, u]
                    elif dz == 2:
                        rows = far[half][dc][block, u]
                    else:
                        source = own if (dx, dz, dc) == (0, 0, 0) else gathered[dx, dz, dc]
                        rows = source[block * PER + t]
                    xa[at : at + 16, :] = rows

    def alpha_dot(*lanes):
        depth = pl.ds(lanes[0] * CAP_A * BLK, len(lanes) * CAP_A * BLK)
        return jnp.dot(wa[:, depth], xa[depth, :], preferred_element_type=jnp.float32)

    def add_alpha(*lanes):
        acc[...] += alpha_dot(*lanes)

    def add_beta():
        acc[...] += lax.dot_general(
            xb[...], wb[...], (((1,), (1,)), ((), ())), preferred_element_type=jnp.float32
        )

    def alpha_chip(dx, dz):
        alpha_weights(dx, dz)
        alpha_inputs(dx, dz, 0, 1)
        add_alpha(0, 1)

    def beta_owner(q, dy):
        owner = beta_at(q, 4 - dy)
        for s in range(CAP_B):
            pick = tab[SEL_B + 8 * s + y, owner * RB]
            for r in range(RB):
                wb[r * BLK : (r + 1) * BLK, s * BLK : (s + 1) * BLK] = bblk[r, tab[INV_B + y * RB + r, pick]]
            column = slice(s * BLK, (s + 1) * BLK)
            if dy:
                xb[:, column] = message[q, dy][s]
            elif q:
                for h in range(2):
                    xb[pl.ds(PARTS[h][0] * 16, PARTS[h][1] * 16), column] = peer_cb[h][pick % RB]
            else:
                xb[:, column] = own_cb[pick % RB]
        add_beta()

    def arrived(copies):
        for copy in copies:
            copy.wait_recv()

    stage_own()
    for r in range(RB):
        bblk[r, SLOTS] = jnp.zeros((BLK, BLK), jnp.bfloat16)
    send_own()
    load_d.wait()

    def init(n, carry):
        at = pl.ds(pl.multiple_of(n * 64, 64), 64)
        acc[at, :] = diag[at, :] * own[pl.ds(n * 4, 4)].astype(jnp.float32).reshape(64, COLS)
        return carry

    lax.fori_loop(0, ROWS // 64, init, 0)
    load_b.wait()
    load_a.wait()
    beta_owner(0, 0)
    arrived(sib[0, 0])
    alpha_chip(0, 0)

    xo = {}

    def over_x(p):
        h = int(p in ("f0", "f1"))
        first, size = PIECES[p]
        xi[p].wait_recv()
        xo[p] = send("xo", part(gathered[1, 0, 0], p), peer[h].at[pl.ds(first - PARTS[h][0], size)])

    zx, zfar, xleaf, zleaf = {}, {}, {}, {}

    def relay(half):
        for i in range(2):
            for dz, block in ((1, 2 + i), (3, i)):
                rows = gathered[0, dz, 0].at[pl.ds(block * PER + half * (PER // 2), PER // 2)]
                zfar[half, block] = send(f"z{dz}", rows, far[half][0].at[block])

    def far_to_sibling(half):
        for block in (2, 0, 3, 1):
            zfar[half, block].wait_recv()
            copy = send("s", far[half][0].at[block], far[half][1].at[block])
            sib.setdefault((0, 2, half), []).append(copy)

    def after(copies, dx, dz, *pieces):
        for p in pieces:
            copies[dz, p].wait_recv()
            to_sibling(dx, dz, p)

    def x_after_z(dz, p):
        zx[dz, p] = send("xi", part(gathered[0, dz, 0], p), part(gathered[1, dz, 0], p))

    def picked_for(link, s, dx, dz, dc):
        return tab[SEL_NEAR[link] + 8 * s, alpha_at(dx, 4 - dz, dc) * RA] % RA

    def stage_x():
        for dc in range(2):
            for s in range(CAP_A):
                block = picked_for("xi", s, 0, 2, dc)
                for t in range(PER // 2):
                    pick_x[dc][s, t] = far[1][dc][block, t]

    def send_x():
        for dc in range(2):
            xleaf[dc] = send("xi", pick_x[dc], leaf_x[dc])

    def stage_z(dc):
        dz = (1, 3)[dc]
        for s in range(CAP_A):
            first = picked_for(f"z{dz}", s, 1, dz, dc) * PER
            for t in range(PER // 2):
                pick_z[dc][s, t] = gathered[1, dz, dc][first + t]

    def send_z(dc):
        zleaf[dc] = send(f"z{(1, 3)[dc]}", pick_z[dc], leaf_z[dc])

    def over_x(p):
        h = int(p in ("f0", "f1"))
        first, size = PIECES[p]
        xi[p].wait_recv()
        xo[p] = send("xo", part(gathered[1, 0, 0], p), peer[h].at[pl.ds(first - PARTS[h][0], size)])

    over_x("n0")
    after(zo, 0, 1, "f")
    x_after_z(1, "f0")
    after(zo, 0, 3, "n")
    relay(1)
    over_x("n1")
    for dz in (1, 3):
        zx[dz, "n"] = send(f"z{dz}", part(gathered[1, 0, 0], "n"), part(gathered[1, dz, 0], "n"))
    to_sibling(1, 0, "n")
    over_x("f0")
    arrived([xo["n0"], xo["n1"]])
    by_column(peer[0], peer_cb[0], PARTS[0][1])
    stage_peer(0)
    arrived(sent_b[0, 2])
    beta_owner(0, 2)
    send_peer(0)
    after(zo, 0, 3, "f")
    x_after_z(3, "f")
    x_after_z(1, "f1")
    after(zo, 0, 1, "n")
    relay(0)
    over_x("f1")
    to_sibling(1, 0, "f")
    arrived(sent_b[0, 1])
    beta_owner(0, 1)
    arrived(sent_b[0, 3])
    beta_owner(0, 3)
    far_to_sibling(1)
    after(zx, 1, 1, "f0")
    arrived([xo["f0"], xo["f1"]])
    by_column(peer[1], peer_cb[1], PARTS[1][1])
    stage_peer(1)
    arrived(sib[0, 2, 1])
    stage_x()
    send_peer(1)
    arrived(sib[1, 0])
    alpha_chip(1, 0)
    send_x()
    arrived(sib[0, 1])
    alpha_chip(0, 1)
    beta_owner(1, 0)
    arrived(sib[0, 3])
    alpha_chip(0, 3)
    after(zx, 1, 3, "f", "n")
    after(zx, 1, 1, "n")
    arrived(sib[1, 3])
    stage_z(1)
    alpha_weights(1, 3)
    send_z(1)
    alpha_inputs(1, 3, 0, 1)
    add_alpha(0, 1)
    after(zx, 1, 1, "f1")
    stage_z(0)
    alpha_weights(1, 1)
    send_z(0)
    arrived(sib[1, 1])
    alpha_inputs(1, 1, 0, 1)
    add_alpha(0, 1)
    far_to_sibling(0)
    arrived(sib[0, 2, 0])
    alpha_chip(0, 2)
    arrived(sent_b[1, 2])
    beta_owner(1, 2)
    arrived(sent_b[1, 1])
    beta_owner(1, 1)
    arrived(sent_b[1, 3])
    beta_owner(1, 3)
    alpha_weights(1, 2)
    arrived([zleaf[0], xleaf[0]])
    alpha_inputs(1, 2, 0)
    add_alpha(0)
    arrived([zleaf[1], xleaf[1]])
    alpha_inputs(1, 2, 1)

    out_ref[...] = (acc[...] + alpha_dot(1)).astype(jnp.bfloat16)
    for copy in started:
        copy.wait_send()
    assert len(started) <= NSEM, len(started)


def per_device(coefficients, diagonal, alpha_blocks, alpha_lists, beta_blocks, beta_lists):
    grouped = pltpu.VMEM((GROUPS, 16, COLS), jnp.bfloat16)
    halves = pltpu.VMEM((RA, PER // 2, 16, COLS), jnp.bfloat16)
    picked = pltpu.VMEM((CAP_A, PER // 2, 16, COLS), jnp.bfloat16)
    by_block = pltpu.VMEM((RB, ROWS, BLK), jnp.bfloat16)
    slots = pltpu.VMEM((CAP_B, ROWS, BLK), jnp.bfloat16)
    scratch = [grouped, by_block] + [grouped] * 11 + [halves] * 4 + [picked] * 8 + [pltpu.VMEM((n, 16, COLS), jnp.bfloat16) for _, n in PARTS]
    scratch += [pltpu.VMEM((RB, n * 16, BLK), jnp.bfloat16) for _, n in PARTS] + [slots] * 12
    scratch += [
        pltpu.VMEM((SLOTS, 64), jnp.int32),
        pltpu.VMEM((SLOTS, 64), jnp.int32),
        pltpu.VMEM((64, SLOTS), jnp.int32),
        pltpu.VMEM((64, SLOTS), jnp.int32),
        pltpu.VMEM((TABLE, BLK), jnp.int32),
        pltpu.SMEM((TABLE, BLK), jnp.int32),
        pltpu.VMEM((RA, SLOTS + 1, BLK, BLK), jnp.bfloat16),
        pltpu.VMEM((RB, SLOTS + 1, BLK, BLK), jnp.bfloat16),
        pltpu.VMEM((ROWS, COLS), jnp.float32),
        pltpu.VMEM((ROWS, COLS), jnp.float32),
        pltpu.VMEM((ROWS, 4 * BLK), jnp.bfloat16),
        pltpu.VMEM((COLS, 4 * BLK), jnp.bfloat16),
        pltpu.VMEM((4 * BLK, COLS), jnp.bfloat16),
        pltpu.VMEM((ROWS, 4 * BLK), jnp.bfloat16),
        pltpu.SemaphoreType.DMA((NSEM,)),
        pltpu.SemaphoreType.DMA((NSEM,)),
        pltpu.SemaphoreType.DMA((7,)),
    ]
    return pl.pallas_call(
        body,
        out_shape=pltpu.VMEM((ROWS, COLS), jnp.bfloat16),
        in_specs=[pl.BlockSpec(memory_space=pl.ANY)] * 6,
        out_specs=pl.BlockSpec(memory_space=pltpu.VMEM),
        scratch_shapes=scratch,
        compiler_params=pltpu.CompilerParams(
            collective_id=0, has_side_effects=True, vmem_limit_bytes=60 * 1024 * 1024
        ),
    )(
        alpha_lists.T,
        beta_lists.T,
        coefficients.reshape(GROUPS, 16, COLS),
        diagonal,
        alpha_blocks,
        beta_blocks,
    )


def solution(mesh):
    in_specs = (
        P("alpha", "beta"),
        P("alpha", "beta"),
        P("alpha", None, None, None),
        P(),
        P("beta", None, None, None),
        P(),
    )
    return jax.shard_map(
        per_device, mesh=mesh, in_specs=in_specs, out_specs=P("alpha", "beta"), check_vma=False
    )
```
